512 devices in a mesh: chan: 32 (over z, y_hi), seg: 16 (over x, y_lo, core).
Axes of the slice: x: 4, y: 8 (y_hi: 4, y_lo: 2; y = y_hi * 2 + y_lo), z: 8, core: 2. Of those that a mesh axis runs over, the one named last changes fastest.
Arguments:
- strain: float32 [1024, 40000], P('chan', 'seg')
- source_channels: int32 [32], replicated, may hold values from 0 to 1023, as said below
Outputs:
- stack: float32 [32, 1024, 501], P('seg', 'chan')
The draws below stay inside these ranges and needn't reach their ends.
Inputs may be any that keep to these rules, and one draw needn't show every extreme that they name: `source_channels`: distinct channels; channel 0 and channel 1024 - 1 are always among them.
All inputs are finite; a program needn't handle non-finite values.
Results may differ from the reference program's by a relative error of at most 0.0001.
Values sent between devices are 32-bit elements; how exact they have to be, the bound alone decides.
A program may use at most 64 MiB of HBM per device.

```python
import math
import jax
import jax.numpy as jnp
from jax import lax

SEG_LEN = 625
TAPS = 63
MAXLAG = 250
SOURCES = 32
SEGMENTS = 16
FIBRE_SENSORS = 1024
UNFILTERED_TICKS = 40000


def draw_strain(key, part):
    generator_seeds = jax.random.split(key, 3)
    array_extents = (FIBRE_SENSORS, UNFILTERED_TICKS)
    background_wavefield = jax.random.normal(generator_seeds[0], array_extents, jnp.float32)
    sensor_amplitude = jnp.exp(jax.random.uniform(generator_seeds[1], (FIBRE_SENSORS, 1), jnp.float32, 0.0, math.log(10.0)))
    seismic_record = jnp.exp(jax.random.uniform(generator_seeds[2], (FIBRE_SENSORS, UNFILTERED_TICKS // 4, 1), jnp.float32, 0.0, math.log(4.0)))
    seismic_record = jnp.broadcast_to(seismic_record, (FIBRE_SENSORS, UNFILTERED_TICKS // 4, 4)).reshape(array_extents)
    return background_wavefield * sensor_amplitude * seismic_record


def draw_source_channels(key, part):
    generator_seeds = jax.random.split(key, 2)
    inner = jax.random.permutation(generator_seeds[0], FIBRE_SENSORS - 2)[:SOURCES - 2].astype(jnp.int32) + 1
    chosen = jnp.concatenate([jnp.array([0, FIBRE_SENSORS - 1], jnp.int32), inner])
    order = jax.random.permutation(generator_seeds[1], SOURCES)
    return chosen[order]


def setup_inputs(seed: int = 0) -> dict:
    key_list = jax.random.split(jax.random.key(seed), 3)
    return {
        "strain": draw_strain(jax.random.fold_in(key_list[2], 71), 0),
        "source_channels": draw_source_channels(jax.random.fold_in(key_list[2], 71), 0),
    }


cutoff = 0.1
water_level = 0.5
epsilon = 1e-06

def tap_shape(position, count):
    window = 0.54 - 0.46 * jnp.cos(2.0 * math.pi * position / (count - 1))
    return window * 2.0 * cutoff * jnp.sinc(2.0 * cutoff * (position - (count - 1) / 2.0))

def whiten(traces):
    spectrum = jnp.fft.rfft(traces, n=2 * SEG_LEN, axis=-1)
    real_part = jnp.real(spectrum).astype(jnp.float32)
    imag_part = jnp.imag(spectrum).astype(jnp.float32)
    power = real_part * real_part + imag_part * imag_part
    bin_span = power.shape[1]
    padded = jnp.pad(power, ((0, 0), (2, 2)))
    smooth = (padded[:, 0:bin_span] + padded[:, 1:bin_span + 1] + padded[:, 2:bin_span + 2] + padded[:, 3:bin_span + 3] + padded[:, 4:bin_span + 4]) / 5.0
    floor_level = water_level * lax.optimization_barrier(jnp.mean(power, axis=1, keepdims=True))
    inverse_norm = 1.0 / jnp.sqrt(jnp.maximum(smooth, floor_level) + epsilon)
    return (real_part * inverse_norm, imag_part * inverse_norm)

def reference(strain, source_channels):
    position = jnp.arange(TAPS).astype(jnp.float32)
    shaped = tap_shape(position, TAPS)
    filter_taps = shaped / jnp.sum(shaped)
    outputs = SEGMENTS * SEG_LEN
    margin = TAPS - 3
    extended = jnp.concatenate([jnp.zeros((FIBRE_SENSORS, margin), jnp.float32), strain], axis=1)
    decimated = jnp.zeros((FIBRE_SENSORS, outputs), jnp.float32)
    for offset in range(TAPS):
        decimated = decimated + filter_taps[TAPS - 1 - offset] * extended[:, offset:offset + 4 * (outputs - 1) + 1:4]
    segments_first = decimated.reshape(FIBRE_SENSORS, SEGMENTS, SEG_LEN).transpose(1, 0, 2)
    fft_length = 2 * SEG_LEN

    def one_segment(running, traces):
        white_re, white_im = whiten(traces)
        src_re = white_re[source_channels]
        src_im = white_im[source_channels]
        cross_re = src_re[:, None, :] * white_re[None, :, :] + src_im[:, None, :] * white_im[None, :, :]
        cross_im = src_re[:, None, :] * white_im[None, :, :] - src_im[:, None, :] * white_re[None, :, :]
        circular = jnp.fft.irfft(lax.complex(cross_re, cross_im), n=fft_length, axis=-1)
        lagged = jnp.concatenate([circular[:, :, fft_length - MAXLAG:], circular[:, :, :MAXLAG + 1]], axis=2)
        return (running + lagged.astype(jnp.float32) * math.sqrt(fft_length), None)
    initial = jnp.zeros((SOURCES, FIBRE_SENSORS, 2 * MAXLAG + 1), jnp.float32)
    summed, unused = lax.scan(one_segment, initial, segments_first)
    return summed / math.sqrt(SEGMENTS)
```

```python
import math

import jax
import jax.numpy as jnp
import ml_dtypes
import numpy as np
from jax import lax
from jax.experimental import pallas as pl
from jax.experimental.pallas import tpu as pltpu
from jax.sharding import PartitionSpec as P

SEG_LEN = 625
TAPS = 63
MAXLAG = 250
SEGS = 16
SOURCES = 32
ROWS = 32
WIDE = 640
RAW = 2500
NZ, NYH, NX = 8, 4, 4

cutoff = 0.1
water_level = 0.5
epsilon = 1e-06

MESH = pl.DeviceIdType.MESH
f32 = jnp.float32
bf16 = jnp.bfloat16


def split_table(table):
    high = table.astype(np.float32).astype(ml_dtypes.bfloat16)
    low = (table - high.astype(np.float64)).astype(np.float32).astype(ml_dtypes.bfloat16)
    return np.stack([high, low])


def band_table():
    position = np.arange(TAPS, dtype=np.float64)
    window = 0.54 - 0.46 * np.cos(2.0 * math.pi * position / (TAPS - 1))
    taps = window * 2.0 * cutoff * np.sinc(2.0 * cutoff * (position - (TAPS - 1) / 2.0))
    taps = taps / taps.sum()
    index = 4 * np.arange(128)[None, :] + 130 - np.arange(WIDE)[:, None]
    valid = (index >= 0) & (index < TAPS)
    return split_table(np.where(valid, taps[np.clip(index, 0, TAPS - 1)], 0.0))


def forward_table():
    samples = np.arange(WIDE)[:, None]
    freqs = np.arange(WIDE)[None, :]
    phase = ((samples * freqs) % (2 * SEG_LEN)) * (math.pi / SEG_LEN)
    valid = (freqs <= SEG_LEN) & (samples < SEG_LEN)
    table = np.concatenate(
        [np.where(valid, np.cos(phase), 0.0), np.where(valid, -np.sin(phase), 0.0)], axis=1
    )
    return split_table(table)


def split(value):
    high = value.astype(bf16)
    return high, (value - high.astype(f32)).astype(bf16)


def dot(a, b):
    return jnp.dot(a, b, preferred_element_type=f32)


def dot_t(a, b):
    return lax.dot_general(a, b, (((1,), (1,)), ((), ())), preferred_element_type=f32)


def whiten(real_part, imag_part):
    power = real_part * real_part + imag_part * imag_part
    near = power + pltpu.roll(power, 1, 1) + pltpu.roll(power, WIDE - 1, 1)
    smooth = (near + pltpu.roll(power, 2, 1) + pltpu.roll(power, WIDE - 2, 1)) / 5.0
    floor_level = (water_level / (SEG_LEN + 1)) * jnp.sum(power, axis=1, keepdims=True)
    inverse_norm = 1.0 / jnp.sqrt(jnp.maximum(smooth, floor_level) + epsilon)
    return real_part * inverse_norm, imag_part * inverse_norm


def kernel(
    strain, channels, band, table, out,
    raw_high, raw_low, traces, pick, first, second, sources,
    trace_high, trace_low, spec, src_rows, src_spec, cross, table_v,
    table_sem, ag_send, ag_recv, p1_send, p1_recv, p2_send, p2_recv, p3_send, p3_recv,
):
    chan = lax.axis_index("chan")
    seg = lax.axis_index("seg")
    z, yh = chan // NYH, chan % NYH
    x, yl, core = seg // 4, (seg // 2) % 2, seg % 2
    half = seg // 2

    def at(chan_index, seg_index):
        return (chan_index, seg_index)

    def seg_of(x_, yl_, core_):
        return (x_ * 2 + yl_) * 2 + core_

    y_peer = at(chan, seg_of(x, 1 - yl, core))
    core_peer = at(chan, seg_of(x, yl, 1 - core))
    self_exchange = lax.rem(2 * half, NZ) == z

    barrier = pltpu.get_barrier_semaphore()

    def greet(device):
        pl.semaphore_signal(barrier, inc=1, device_id=device, device_id_type=MESH)

    greet(y_peer)
    greet(core_peer)
    for d in range(1, NX):
        greet(at(chan, seg_of(lax.rem(x + d, NX), yl, core)))
    for d in range(1, NYH):
        greet(at(z * NYH + lax.rem(yh + d, NYH), seg))
    for d in range(1, NZ):
        greet(at(lax.rem(z + d, NZ) * NYH + yh, seg))
    q = lax.rem(z - half + NZ, NZ)

    def greet_first(i, carry):
        zs, gs = i // 2, 2 * q + i % 2

        @pl.when(jnp.logical_not((zs == z) & (gs == seg)))
        def _():
            greet(at(zs * NYH + yh, gs))

        return carry

    lax.fori_loop(0, 16, greet_first, 0)

    table_copy = pltpu.make_async_copy(table, table_v, table_sem)
    table_copy.start()

    for ref, part in ((raw_high, 0), (raw_low, 1)):
        ref[:, 0:128] = jnp.zeros((ROWS, 128), bf16)
        ref[:, 2560:2688] = jnp.zeros((ROWS, 128), bf16)
    body = split(strain[:, 0:2432])
    tail = split(strain[:, 2432:RAW])
    raw_high[:, 128:2560] = body[0]
    raw_low[:, 128:2560] = body[1]
    raw_high[:, 2560 : 2560 + 68] = tail[0]
    raw_low[:, 2560 : 2560 + 68] = tail[1]
    win_high = jnp.concatenate([raw_high[:, 512 * b : 512 * b + WIDE] for b in range(5)], axis=0)
    win_low = jnp.concatenate([raw_low[:, 512 * b : 512 * b + WIDE] for b in range(5)], axis=0)
    both = dot(jnp.concatenate([win_high, win_low], axis=0), band[0])
    dec = both[0:160] + both[160:320] + dot(win_high, band[1])
    dec = jnp.concatenate([dec[32 * b : 32 * b + 32] for b in range(5)], axis=1)
    traces[seg] = dec

    local = channels[...] - chan * ROWS
    onehot_t = (lax.broadcasted_iota(jnp.int32, (ROWS, SOURCES), 0) == local).astype(f32)
    picked = lax.dot_general(
        onehot_t, dec, (((0,), (0,)), ((), ())),
        precision=lax.Precision.HIGHEST, preferred_element_type=f32,
    )
    for j in range(SEGS):
        pick[j] = picked[2 * j : 2 * j + 2]

    @pl.when(self_exchange)
    def _():
        pl.semaphore_wait(barrier, 2 + 3 + 3 + 7 + 15)

    @pl.when(jnp.logical_not(self_exchange))
    def _():
        pl.semaphore_wait(barrier, 2 + 3 + 3 + 7 + 16)

    def first_copy(j):
        zd = lax.rem(half + j // 2, NZ)
        slot = z * 2 + core
        return pltpu.make_async_remote_copy(
            src_ref=pick.at[j], dst_ref=first.at[slot],
            send_sem=p1_send.at[j], recv_sem=p1_recv.at[slot],
            device_id=at(zd * NYH + yh, j), device_id_type=MESH,
        )

    def is_self(j):
        return self_exchange & (j == seg)

    def send_first(i, carry):
        j = lax.rem(seg + i, SEGS)

        @pl.when(jnp.logical_not(is_self(j)))
        def _():
            first_copy(j).start()

        return carry

    lax.fori_loop(0, SEGS, send_first, 0)

    @pl.when(self_exchange)
    def _():
        first[z * 2 + core] = pick[seg]

    def ag_copy(slot, index, device):
        return pltpu.make_async_remote_copy(
            src_ref=traces.at[slot], dst_ref=traces.at[slot],
            send_sem=ag_send.at[index], recv_sem=ag_recv.at[slot],
            device_id=device, device_id_type=MESH,
        )

    started = []

    def ag_start(slot, index, device):
        copy = ag_copy(slot, index, device)
        copy.start()
        started.append(copy)

    ag_start(seg, 3, y_peer)
    for d in (1, 3, 2):
        ag_start(seg, d - 1, at(chan, seg_of(lax.rem(x + d, NX), yl, core)))
    ag_start(seg, 7, core_peer)

    def ag_wait(slot):
        ag_copy(slot, 0, core_peer).wait_recv()

    def from_y(d):
        slot = seg_of(lax.rem(x + d, NX), 1 - yl, core)
        ag_wait(slot)
        ag_start(slot, 11 + d, core_peer)

    for d in (3, 1, 2):
        slot = seg_of(lax.rem(x + d, NX), yl, core)
        ag_wait(slot)
        ag_start(slot, 3 + d, y_peer)
        ag_start(slot, 7 + d, core_peer)

    def wait_first(i, carry):
        zs, gs = i // 2, 2 * q + i % 2

        @pl.when(jnp.logical_not((zs == z) & (gs == seg)))
        def _():
            pltpu.make_async_remote_copy(
                src_ref=pick.at[0], dst_ref=first.at[i],
                send_sem=p1_send.at[0], recv_sem=p1_recv.at[i],
                device_id=core_peer, device_id_type=MESH,
            ).wait_recv()

        return carry

    lax.fori_loop(0, 16, wait_first, 0)
    for low in range(2):
        total = first[low]
        for zs in range(1, NZ):
            total = total + first[2 * zs + low]
        second[yh, low] = total

    def second_copy(d):
        return pltpu.make_async_remote_copy(
            src_ref=second.at[yh], dst_ref=second.at[yh],
            send_sem=p2_send.at[d], recv_sem=p2_recv.at[yh],
            device_id=at(z * NYH + lax.rem(yh + d, NYH), seg), device_id_type=MESH,
        )

    for d in (2, 1, 3):
        copy = second_copy(d)
        copy.start()
        started.append(copy)

    for d in (0, 3, 1, 2):
        from_y(d)

    for d in range(1, NYH):
        slot = lax.rem(yh + d, NYH)
        pltpu.make_async_remote_copy(
            src_ref=second.at[slot], dst_ref=second.at[slot],
            send_sem=p2_send.at[d], recv_sem=p2_recv.at[slot],
            device_id=core_peer, device_id_type=MESH,
        ).wait_recv()
    for low in range(2):
        sources[q, low] = second[0, low] + second[1, low] + second[2, low] + second[3, low]

    def third_copy(slot, index, device):
        return pltpu.make_async_remote_copy(
            src_ref=sources.at[slot], dst_ref=sources.at[slot],
            send_sem=p3_send.at[index], recv_sem=p3_recv.at[slot],
            device_id=device, device_id_type=MESH,
        )

    for d in (4, 3, 5, 2, 6, 1, 7):
        copy = third_copy(q, d, at(lax.rem(z + d, NZ) * NYH + yh, seg))
        copy.start()
        started.append(copy)

    for x_ in range(NX):
        for yl_ in range(2):
            ag_wait(seg_of(x_, yl_, 1 - core))

    table_copy.wait()

    lane = lax.broadcasted_iota(jnp.int32, (ROWS, 128), 1)

    def prepare(g, carry):
        before = jnp.maximum(g - 1, 0)
        spill = pltpu.roll(traces[before, :, 512:640], 15, 1)
        head = traces[g, :, 0:128] + jnp.where((lane < 15) & (g > 0), spill, 0.0)
        rows = pl.ds(pl.multiple_of(g * ROWS, ROWS), ROWS)
        trace_high[rows, 0:128], trace_low[rows, 0:128] = split(head)
        trace_high[rows, 128:640], trace_low[rows, 128:640] = split(traces[g, :, 128:640])
        return carry

    lax.fori_loop(0, SEGS, prepare, 0)

    def transform(block, carry):
        rows = pl.ds(pl.multiple_of((block // 5) * 256, 256), 256)
        cols = pl.ds(pl.multiple_of((block % 5) * 256, 256), 256)
        high = trace_high[rows, :]
        t_high = table_v[0, :, cols]
        spec[rows, cols] = (
            dot(high, t_high) + dot(trace_low[rows, :], t_high) + dot(high, table_v[1, :, cols])
        )
        return carry

    lax.fori_loop(0, 10, transform, 0)

    def whiten_rows(g, carry):
        rows = pl.ds(pl.multiple_of(g * ROWS, ROWS), ROWS)
        re, im = whiten(spec[rows, 0:640], spec[rows, 640:1280])
        spec[rows, 0:640] = re
        spec[rows, 640:1280] = im
        return carry

    lax.fori_loop(0, SEGS, whiten_rows, 0)

    for d in range(1, NZ):
        slot = lax.rem(q + d, NZ)
        third_copy(slot, 0, core_peer).wait_recv()
    for g in range(SEGS):
        for e in range(2):
            src_rows[e * 16 + g : e * 16 + g + 1, :] = sources[g // 2, g % 2, e : e + 1, :]
    lane16 = lax.broadcasted_iota(jnp.int32, (16, 128), 1)
    row16 = lax.broadcasted_iota(jnp.int32, (16, 128), 0)
    heads = []
    for e in range(2):
        spill = pltpu.roll(pltpu.roll(src_rows[e * 16 : e * 16 + 16, 512:640], 15, 1), 1, 0)
        keep = (lane16 < 15) & (row16 > 0)
        heads.append(src_rows[e * 16 : e * 16 + 16, 0:128] + jnp.where(keep, spill, 0.0))
    whole = jnp.concatenate([jnp.concatenate(heads, axis=0), src_rows[:, 128:640]], axis=1)
    s_high, s_low = split(whole)
    s_both = jnp.concatenate([s_high, s_low], axis=0)

    def transform_src(block, carry):
        cols = pl.ds(pl.multiple_of(block * 256, 256), 256)
        pair = dot(s_both, table_v[0, :, cols])
        src_spec[:, cols] = pair[0:32] + pair[32:64] + dot(s_high, table_v[1, :, cols])
        return carry

    lax.fori_loop(0, 5, transform_src, 0)
    re, im = whiten(src_spec[:, 0:640], src_spec[:, 640:1280])
    src_spec[:, 0:640] = re
    src_spec[:, 640:1280] = im

    factor = 1.0 / math.sqrt(2.0 * SEG_LEN * SEGS)

    def cross_block(block, carry):
        re_cols = pl.ds(pl.multiple_of(block * 128, 128), 128)
        im_cols = pl.ds(pl.multiple_of(640 + block * 128, 128), 128)
        freq = block * 128 + lane
        weight = jnp.where((freq == 0) | (freq == SEG_LEN), factor, 2.0 * factor)
        acc = [[jnp.zeros((ROWS, 128), f32) for _ in range(2)] for _ in range(2)]
        for g in range(SEGS):
            c_re = spec[g * ROWS : g * ROWS + ROWS, re_cols]
            c_im = spec[g * ROWS : g * ROWS + ROWS, im_cols]
            for e in range(2):
                s_re = src_spec[e * 16 + g : e * 16 + g + 1, re_cols]
                s_im = src_spec[e * 16 + g : e * 16 + g + 1, im_cols]
                acc[e][0] = acc[e][0] + (s_re * c_re + s_im * c_im)
                acc[e][1] = acc[e][1] + (s_re * c_im - s_im * c_re)
        for e in range(2):
            cross[e * ROWS : e * ROWS + ROWS, re_cols] = acc[e][0] * weight
            cross[e * ROWS : e * ROWS + ROWS, im_cols] = acc[e][1] * weight
        return carry

    lax.fori_loop(0, 5, cross_block, 0)

    parts = []
    for base in (0, 640):
        c_high, c_low = split(cross[:, base : base + 640])
        pair = dot_t(jnp.concatenate([c_high, c_low], axis=0), table_v[0, 0:256, base : base + 640])
        parts.append(
            pair[0:64] + pair[64:128] + dot_t(c_high, table_v[1, 0:256, base : base + 640])
        )
    even, odd = parts
    lags = jnp.concatenate([even - odd, even + odd], axis=1)
    l_high, l_low = split(lags)
    l_last = (lags - l_high.astype(f32) - l_low.astype(f32)).astype(bf16)
    row = lax.broadcasted_iota(jnp.int32, (512, 512), 0)
    col = lax.broadcasted_iota(jnp.int32, (512, 512), 1)
    negative = (row > 0) & (row < 256) & (col == MAXLAG - row)
    positive = (row >= 256) & (col == MAXLAG - 256 + row)
    place = jnp.where(negative | positive, 1.0, 0.0).astype(bf16)
    moved = dot(jnp.concatenate([l_high, l_low, l_last], axis=0), place)
    placed = moved[0:64] + moved[64:128] + moved[128:192]
    for e in range(2):
        out[e] = placed[e * ROWS : e * ROWS + ROWS, 0 : 2 * MAXLAG + 1]

    for copy in started:
        copy.wait_send()

    def wait_send_first(j, carry):
        @pl.when(jnp.logical_not(is_self(j)))
        def _():
            first_copy(j).wait_send()

        return carry

    lax.fori_loop(0, SEGS, wait_send_first, 0)


def body(strain, source_channels):
    vmem = pl.BlockSpec(memory_space=pltpu.VMEM)
    sem = pltpu.SemaphoreType.DMA
    return pl.pallas_call(
        kernel,
        out_shape=jax.ShapeDtypeStruct((2, ROWS, 2 * MAXLAG + 1), f32),
        in_specs=[vmem, vmem, vmem, pl.BlockSpec(memory_space=pl.ANY)],
        out_specs=vmem,
        scratch_shapes=[
            pltpu.VMEM((ROWS, 2688), bf16),
            pltpu.VMEM((ROWS, 2688), bf16),
            pltpu.VMEM((SEGS, ROWS, WIDE), f32),
            pltpu.VMEM((SEGS, 2, WIDE), f32),
            pltpu.VMEM((16, 2, WIDE), f32),
            pltpu.VMEM((NYH, 2, 2, WIDE), f32),
            pltpu.VMEM((NZ, 2, 2, WIDE), f32),
            pltpu.VMEM((SEGS * ROWS, WIDE), bf16),
            pltpu.VMEM((SEGS * ROWS, WIDE), bf16),
            pltpu.VMEM((SEGS * ROWS, 2 * WIDE), f32),
            pltpu.VMEM((32, WIDE), f32),
            pltpu.VMEM((32, 2 * WIDE), f32),
            pltpu.VMEM((64, 2 * WIDE), f32),
            pltpu.VMEM((2, WIDE, 2 * WIDE), bf16),
            sem(()), sem((16,)), sem((16,)), sem((16,)), sem((16,)),
            sem((4,)), sem((4,)), sem((8,)), sem((8,)),
        ],
        compiler_params=pltpu.CompilerParams(collective_id=0, has_side_effects=True),
        name="noise_stack",
    )(strain, source_channels.reshape(1, SOURCES), jnp.asarray(band_table()), jnp.asarray(forward_table()))


def solution(mesh):
    in_specs = (P("chan", "seg"), P())
    out_specs = P("seg", "chan", None)
    return jax.shard_map(body, mesh=mesh, in_specs=in_specs, out_specs=out_specs, check_vma=False)
```

```python
import math

import jax
import jax.numpy as jnp
import ml_dtypes
import numpy as np
from jax import lax
from jax.experimental import pallas as pl
from jax.experimental.pallas import tpu as pltpu
from jax.sharding import PartitionSpec as P

SEG_LEN = 625
TAPS = 63
MAXLAG = 250
SEGS = 16
SOURCES = 32
ROWS = 32
WIDE = 640
RAW = 2500
NZ, NYH, NX = 8, 4, 4

cutoff = 0.1
water_level = 0.5
epsilon = 1e-06

MESH = pl.DeviceIdType.MESH
f32 = jnp.float32
bf16 = jnp.bfloat16


def split_table(table):
    high = table.astype(np.float32).astype(ml_dtypes.bfloat16)
    low = (table - high.astype(np.float64)).astype(np.float32).astype(ml_dtypes.bfloat16)
    return np.stack([high, low])


def band_table():
    position = np.arange(TAPS, dtype=np.float64)
    window = 0.54 - 0.46 * np.cos(2.0 * math.pi * position / (TAPS - 1))
    taps = window * 2.0 * cutoff * np.sinc(2.0 * cutoff * (position - (TAPS - 1) / 2.0))
    taps = taps / taps.sum()
    index = 4 * np.arange(128)[None, :] + 130 - np.arange(WIDE)[:, None]
    valid = (index >= 0) & (index < TAPS)
    return split_table(np.where(valid, taps[np.clip(index, 0, TAPS - 1)], 0.0))


def forward_table():
    samples = np.arange(WIDE)[:, None]
    freqs = np.arange(WIDE)[None, :]
    phase = ((samples * freqs) % (2 * SEG_LEN)) * (math.pi / SEG_LEN)
    valid = (freqs <= SEG_LEN) & (samples < SEG_LEN)
    table = np.concatenate(
        [np.where(valid, np.cos(phase), 0.0), np.where(valid, -np.sin(phase), 0.0)], axis=1
    )
    return split_table(table)


def split(value):
    high = value.astype(bf16)
    return high, (value - high.astype(f32)).astype(bf16)


def dot(a, b):
    return jnp.dot(a, b, preferred_element_type=f32)


def dot_t(a, b):
    return lax.dot_general(a, b, (((1,), (1,)), ((), ())), preferred_element_type=f32)


def whiten(real_part, imag_part):
    power = real_part * real_part + imag_part * imag_part
    near = power + pltpu.roll(power, 1, 1) + pltpu.roll(power, WIDE - 1, 1)
    smooth = (near + pltpu.roll(power, 2, 1) + pltpu.roll(power, WIDE - 2, 1)) * 0.2
    floor_level = (water_level / (SEG_LEN + 1)) * jnp.sum(power, axis=1, keepdims=True)
    inverse_norm = lax.rsqrt(jnp.maximum(smooth, floor_level) + epsilon)
    return real_part * inverse_norm, imag_part * inverse_norm


def kernel(
    strain, channels, band, table, out,
    raw_high, raw_low, traces, pick, first, second, sources,
    trace_parts, spec, src_rows, src_spec, cross, table_v,
    table_sem, ag_send, ag_recv, p1_send, p1_recv, p2_send, p2_recv, p3_send, p3_recv,
):
    chan = lax.axis_index("chan")
    seg = lax.axis_index("seg")
    z, yh = chan // NYH, chan % NYH
    x, yl, core = seg // 4, (seg // 2) % 2, seg % 2
    half = seg // 2

    def at(chan_index, seg_index):
        return (chan_index, seg_index)

    def seg_of(x_, yl_, core_):
        return (x_ * 2 + yl_) * 2 + core_

    y_peer = at(chan, seg_of(x, 1 - yl, core))
    core_peer = at(chan, seg_of(x, yl, 1 - core))
    self_exchange = lax.rem(2 * half, NZ) == z

    barrier = pltpu.get_barrier_semaphore()

    def greet(device):
        pl.semaphore_signal(barrier, inc=1, device_id=device, device_id_type=MESH)

    greet(y_peer)
    greet(core_peer)
    for d in range(1, NX):
        greet(at(chan, seg_of(lax.rem(x + d, NX), yl, core)))
    for d in range(1, NYH):
        greet(at(z * NYH + lax.rem(yh + d, NYH), seg))
    for d in range(1, NZ):
        greet(at(lax.rem(z + d, NZ) * NYH + yh, seg))
    q = lax.rem(z - half + NZ, NZ)

    def greet_first(i, carry):
        zs, gs = i // 2, 2 * q + i % 2

        @pl.when(jnp.logical_not((zs == z) & (gs == seg)))
        def _():
            greet(at(zs * NYH + yh, gs))

        return carry

    lax.fori_loop(0, 16, greet_first, 0)

    table_copies = []
    for i, part in enumerate((0, 0, 1)):
        copy = pltpu.make_async_copy(
            table.at[part], table_v.at[WIDE * i : WIDE * i + WIDE], table_sem.at[i]
        )
        copy.start()
        table_copies.append(copy)

    for ref, part in ((raw_high, 0), (raw_low, 1)):
        ref[:, 0:128] = jnp.zeros((ROWS, 128), bf16)
        ref[:, 2560:2688] = jnp.zeros((ROWS, 128), bf16)
    body = split(strain[:, 0:2432])
    tail = split(strain[:, 2432:RAW])
    raw_high[:, 128:2560] = body[0]
    raw_low[:, 128:2560] = body[1]
    raw_high[:, 2560 : 2560 + 68] = tail[0]
    raw_low[:, 2560 : 2560 + 68] = tail[1]
    win_high = jnp.concatenate([raw_high[:, 512 * b : 512 * b + WIDE] for b in range(5)], axis=0)
    win_low = jnp.concatenate([raw_low[:, 512 * b : 512 * b + WIDE] for b in range(5)], axis=0)
    both = dot(jnp.concatenate([win_high, win_low], axis=0), band[0])
    dec = both[0:160] + both[160:320] + dot(win_high, band[1])
    dec = jnp.concatenate([dec[32 * b : 32 * b + 32] for b in range(5)], axis=1)
    traces[seg] = dec

    local = channels[...] - chan * ROWS
    onehot_t = (lax.broadcasted_iota(jnp.int32, (ROWS, SOURCES), 0) == local).astype(f32)
    picked = lax.dot_general(
        onehot_t, dec, (((0,), (0,)), ((), ())),
        precision=lax.Precision.HIGHEST, preferred_element_type=f32,
    )
    for j in range(SEGS):
        pick[j] = picked[2 * j : 2 * j + 2]

    @pl.when(self_exchange)
    def _():
        pl.semaphore_wait(barrier, 2 + 3 + 3 + 7 + 15)

    @pl.when(jnp.logical_not(self_exchange))
    def _():
        pl.semaphore_wait(barrier, 2 + 3 + 3 + 7 + 16)

    def first_copy(j):
        zd = lax.rem(half + j // 2, NZ)
        slot = z * 2 + core
        return pltpu.make_async_remote_copy(
            src_ref=pick.at[j], dst_ref=first.at[slot],
            send_sem=p1_send.at[j], recv_sem=p1_recv.at[slot],
            device_id=at(zd * NYH + yh, j), device_id_type=MESH,
        )

    def is_self(j):
        return self_exchange & (j == seg)

    def send_first(i, carry):
        j = lax.rem(seg + i, SEGS)

        @pl.when(jnp.logical_not(is_self(j)))
        def _():
            first_copy(j).start()

        return carry

    lax.fori_loop(0, SEGS, send_first, 0)

    @pl.when(self_exchange)
    def _():
        first[z * 2 + core] = pick[seg]

    def ag_copy(slot, index, device):
        return pltpu.make_async_remote_copy(
            src_ref=traces.at[slot], dst_ref=traces.at[slot],
            send_sem=ag_send.at[index], recv_sem=ag_recv.at[slot],
            device_id=device, device_id_type=MESH,
        )

    started = []

    def ag_start(slot, index, device):
        copy = ag_copy(slot, index, device)
        copy.start()
        started.append(copy)

    ag_start(seg, 3, y_peer)
    for d in (1, 3, 2):
        ag_start(seg, d - 1, at(chan, seg_of(lax.rem(x + d, NX), yl, core)))
    ag_start(seg, 7, core_peer)

    def ag_wait(slot):
        ag_copy(slot, 0, core_peer).wait_recv()

    def from_y(d):
        slot = seg_of(lax.rem(x + d, NX), 1 - yl, core)
        ag_wait(slot)
        ag_start(slot, 11 + d, core_peer)

    for d in (3, 1, 2):
        slot = seg_of(lax.rem(x + d, NX), yl, core)
        ag_wait(slot)
        ag_start(slot, 3 + d, y_peer)
        ag_start(slot, 7 + d, core_peer)

    for d in (0, 3, 1, 2):
        from_y(d)

    for x_ in range(NX):
        for yl_ in range(2):
            ag_wait(seg_of(x_, yl_, 1 - core))

    for copy in table_copies:
        copy.wait()

    lane = lax.broadcasted_iota(jnp.int32, (ROWS, 128), 1)

    def prepare(g, carry):
        before = jnp.maximum(g - 1, 0)
        spill = pltpu.roll(traces[before, :, 512:640], 15, 1)
        head = traces[g, :, 0:128] + jnp.where((lane < 15) & (g > 0), spill, 0.0)
        rows = pl.ds(pl.multiple_of(g * ROWS, ROWS), ROWS)
        for high, low, first_col, last_col in (
            (*split(head), 0, 128),
            (*split(traces[g, :, 128:640]), 128, 640),
        ):
            trace_parts[rows, first_col:last_col] = high
            trace_parts[rows, WIDE + first_col : WIDE + last_col] = low
            trace_parts[rows, 2 * WIDE + first_col : 2 * WIDE + last_col] = high
        return carry

    lax.fori_loop(0, SEGS, prepare, 0)

    def transform(block, carry):
        rows = pl.ds(pl.multiple_of((block // 5) * 256, 256), 256)
        cols = pl.ds(pl.multiple_of((block % 5) * 256, 256), 256)
        spec[rows, cols] = dot(trace_parts[rows, :], table_v[:, cols])
        return carry

    lax.fori_loop(0, 3, transform, 0)

    def wait_first(i, carry):
        zs, gs = i // 2, 2 * q + i % 2

        @pl.when(jnp.logical_not((zs == z) & (gs == seg)))
        def _():
            pltpu.make_async_remote_copy(
                src_ref=pick.at[0], dst_ref=first.at[i],
                send_sem=p1_send.at[0], recv_sem=p1_recv.at[i],
                device_id=core_peer, device_id_type=MESH,
            ).wait_recv()

        return carry

    lax.fori_loop(0, 16, wait_first, 0)
    for low in range(2):
        total = first[low]
        for zs in range(1, NZ):
            total = total + first[2 * zs + low]
        second[yh, low] = total

    def second_copy(d):
        return pltpu.make_async_remote_copy(
            src_ref=second.at[yh], dst_ref=second.at[yh],
            send_sem=p2_send.at[d], recv_sem=p2_recv.at[yh],
            device_id=at(z * NYH + lax.rem(yh + d, NYH), seg), device_id_type=MESH,
        )

    for d in (2, 1, 3):
        copy = second_copy(d)
        copy.start()
        started.append(copy)

    lax.fori_loop(3, 10, transform, 0)

    for d in range(1, NYH):
        slot = lax.rem(yh + d, NYH)
        pltpu.make_async_remote_copy(
            src_ref=second.at[slot], dst_ref=second.at[slot],
            send_sem=p2_send.at[d], recv_sem=p2_recv.at[slot],
            device_id=core_peer, device_id_type=MESH,
        ).wait_recv()
    for low in range(2):
        sources[q, low] = second[0, low] + second[1, low] + second[2, low] + second[3, low]

    def third_copy(slot, index, device):
        return pltpu.make_async_remote_copy(
            src_ref=sources.at[slot], dst_ref=sources.at[slot],
            send_sem=p3_send.at[index], recv_sem=p3_recv.at[slot],
            device_id=device, device_id_type=MESH,
        )

    for d in (4, 3, 5, 2, 6, 1, 7):
        copy = third_copy(q, d, at(lax.rem(z + d, NZ) * NYH + yh, seg))
        copy.start()
        started.append(copy)

    def whiten_rows(g, carry):
        rows = pl.ds(pl.multiple_of(g * ROWS, ROWS), ROWS)
        re, im = whiten(spec[rows, 0:640], spec[rows, 640:1280])
        spec[rows, 0:640] = re
        spec[rows, 640:1280] = im
        return carry

    lax.fori_loop(0, SEGS, whiten_rows, 0)

    for d in range(1, NZ):
        slot = lax.rem(q + d, NZ)
        third_copy(slot, 0, core_peer).wait_recv()
    for g in range(SEGS):
        for e in range(2):
            src_rows[e * 16 + g : e * 16 + g + 1, :] = sources[g // 2, g % 2, e : e + 1, :]
    lane16 = lax.broadcasted_iota(jnp.int32, (16, 128), 1)
    row16 = lax.broadcasted_iota(jnp.int32, (16, 128), 0)
    heads = []
    for e in range(2):
        spill = pltpu.roll(pltpu.roll(src_rows[e * 16 : e * 16 + 16, 512:640], 15, 1), 1, 0)
        keep = (lane16 < 15) & (row16 > 0)
        heads.append(src_rows[e * 16 : e * 16 + 16, 0:128] + jnp.where(keep, spill, 0.0))
    whole = jnp.concatenate([jnp.concatenate(heads, axis=0), src_rows[:, 128:640]], axis=1)
    s_high, s_low = split(whole)
    s_both = jnp.concatenate([s_high, s_low], axis=0)

    def transform_src(block, carry):
        cols = pl.ds(pl.multiple_of(block * 256, 256), 256)
        pair = dot(s_both, table_v[0:WIDE, cols])
        src_spec[:, cols] = pair[0:32] + pair[32:64] + dot(s_high, table_v[2 * WIDE : 3 * WIDE, cols])
        return carry

    lax.fori_loop(0, 5, transform_src, 0)
    re, im = whiten(src_spec[:, 0:640], src_spec[:, 640:1280])
    src_spec[:, 0:640] = re
    src_spec[:, 640:1280] = im

    factor = 1.0 / math.sqrt(2.0 * SEG_LEN * SEGS)

    def cross_block(block, carry):
        re_cols = pl.ds(pl.multiple_of(block * 128, 128), 128)
        im_cols = pl.ds(pl.multiple_of(640 + block * 128, 128), 128)
        freq = block * 128 + lane
        weight = jnp.where((freq == 0) | (freq == SEG_LEN), factor, 2.0 * factor)
        acc = [[jnp.zeros((ROWS, 128), f32) for _ in range(2)] for _ in range(2)]
        for g in range(SEGS):
            c_re = spec[g * ROWS : g * ROWS + ROWS, re_cols]
            c_im = spec[g * ROWS : g * ROWS + ROWS, im_cols]
            for e in range(2):
                s_re = src_spec[e * 16 + g : e * 16 + g + 1, re_cols]
                s_im = src_spec[e * 16 + g : e * 16 + g + 1, im_cols]
                acc[e][0] = acc[e][0] + (s_re * c_re + s_im * c_im)
                acc[e][1] = acc[e][1] + (s_re * c_im - s_im * c_re)
        for e in range(2):
            cross[e * ROWS : e * ROWS + ROWS, re_cols] = acc[e][0] * weight
            cross[e * ROWS : e * ROWS + ROWS, im_cols] = acc[e][1] * weight
        return carry

    lax.fori_loop(0, 5, cross_block, 0)

    parts = []
    for base in (0, 640):
        c_high, c_low = split(cross[:, base : base + 640])
        pair = dot_t(jnp.concatenate([c_high, c_low], axis=0), table_v[0:256, base : base + 640])
        parts.append(
            pair[0:64] + pair[64:128] + dot_t(c_high, table_v[2 * WIDE : 2 * WIDE + 256, base : base + 640])
        )
    even, odd = parts
    lags = jnp.concatenate([even - odd, even + odd], axis=1)
    l_high, l_low = split(lags)
    l_last = (lags - l_high.astype(f32) - l_low.astype(f32)).astype(bf16)
    row = lax.broadcasted_iota(jnp.int32, (512, 512), 0)
    col = lax.broadcasted_iota(jnp.int32, (512, 512), 1)
    negative = (row > 0) & (row < 256) & (col == MAXLAG - row)
    positive = (row >= 256) & (col == MAXLAG - 256 + row)
    place = jnp.where(negative | positive, 1.0, 0.0).astype(bf16)
    moved = dot(jnp.concatenate([l_high, l_low, l_last], axis=0), place)
    placed = moved[0:64] + moved[64:128] + moved[128:192]
    for e in range(2):
        out[e] = placed[e * ROWS : e * ROWS + ROWS, 0 : 2 * MAXLAG + 1]

    for copy in started:
        copy.wait_send()

    def wait_send_first(j, carry):
        @pl.when(jnp.logical_not(is_self(j)))
        def _():
            first_copy(j).wait_send()

        return carry

    lax.fori_loop(0, SEGS, wait_send_first, 0)


def body(strain, source_channels):
    vmem = pl.BlockSpec(memory_space=pltpu.VMEM)
    sem = pltpu.SemaphoreType.DMA
    return pl.pallas_call(
        kernel,
        out_shape=jax.ShapeDtypeStruct((2, ROWS, 2 * MAXLAG + 1), f32),
        in_specs=[vmem, vmem, vmem, pl.BlockSpec(memory_space=pl.ANY)],
        out_specs=vmem,
        scratch_shapes=[
            pltpu.VMEM((ROWS, 2688), bf16),
            pltpu.VMEM((ROWS, 2688), bf16),
            pltpu.VMEM((SEGS, ROWS, WIDE), f32),
            pltpu.VMEM((SEGS, 2, WIDE), f32),
            pltpu.VMEM((16, 2, WIDE), f32),
            pltpu.VMEM((NYH, 2, 2, WIDE), f32),
            pltpu.VMEM((NZ, 2, 2, WIDE), f32),
            pltpu.VMEM((SEGS * ROWS, 3 * WIDE), bf16),
            pltpu.VMEM((SEGS * ROWS, 2 * WIDE), f32),
            pltpu.VMEM((32, WIDE), f32),
            pltpu.VMEM((32, 2 * WIDE), f32),
            pltpu.VMEM((64, 2 * WIDE), f32),
            pltpu.VMEM((3 * WIDE, 2 * WIDE), bf16),
            sem((3,)), sem((16,)), sem((16,)), sem((16,)), sem((16,)),
            sem((4,)), sem((4,)), sem((8,)), sem((8,)),
        ],
        compiler_params=pltpu.CompilerParams(collective_id=0, has_side_effects=True),
        name="noise_stack",
    )(strain, source_channels.reshape(1, SOURCES), jnp.asarray(band_table()), jnp.asarray(forward_table()))


def solution(mesh):
    in_specs = (P("chan", "seg"), P())
    out_specs = P("seg", "chan", None)
    return jax.shard_map(body, mesh=mesh, in_specs=in_specs, out_specs=out_specs, check_vma=False)
```

```python
import math

import jax
import jax.numpy as jnp
import ml_dtypes
import numpy as np
from jax import lax
from jax.experimental import pallas as pl
from jax.experimental.pallas import tpu as pltpu
from jax.sharding import PartitionSpec as P

SEG_LEN = 625
TAPS = 63
MAXLAG = 250
SEGS = 16
SOURCES = 32
ROWS = 32
WIDE = 640
RAW = 2500
NZ, NYH, NX = 8, 4, 4

cutoff = 0.1
water_level = 0.5
epsilon = 1e-06

MESH = pl.DeviceIdType.MESH
f32 = jnp.float32
bf16 = jnp.bfloat16


def split_table(table):
    high = table.astype(np.float32).astype(ml_dtypes.bfloat16)
    low = (table - high.astype(np.float64)).astype(np.float32).astype(ml_dtypes.bfloat16)
    return np.stack([high, low])


def band_table():
    position = np.arange(TAPS, dtype=np.float64)
    window = 0.54 - 0.46 * np.cos(2.0 * math.pi * position / (TAPS - 1))
    taps = window * 2.0 * cutoff * np.sinc(2.0 * cutoff * (position - (TAPS - 1) / 2.0))
    taps = taps / taps.sum()
    index = 4 * np.arange(128)[None, :] + 130 - np.arange(WIDE)[:, None]
    valid = (index >= 0) & (index < TAPS)
    return split_table(np.where(valid, taps[np.clip(index, 0, TAPS - 1)], 0.0))


def forward_table():
    samples = np.arange(WIDE)[:, None]
    freqs = np.arange(WIDE)[None, :]
    phase = ((samples * freqs) % (2 * SEG_LEN)) * (math.pi / SEG_LEN)
    valid = (freqs <= SEG_LEN) & (samples < SEG_LEN)
    table = np.concatenate(
        [np.where(valid, np.cos(phase), 0.0), np.where(valid, -np.sin(phase), 0.0)], axis=1
    )
    return split_table(table)


def split(value):
    high = value.astype(bf16)
    return high, (value - high.astype(f32)).astype(bf16)


def dot(a, b):
    return jnp.dot(a, b, preferred_element_type=f32)


def dot_t(a, b):
    return lax.dot_general(a, b, (((1,), (1,)), ((), ())), preferred_element_type=f32)


def whiten(real_part, imag_part):
    power = real_part * real_part + imag_part * imag_part
    near = power + pltpu.roll(power, 1, 1) + pltpu.roll(power, WIDE - 1, 1)
    smooth = (near + pltpu.roll(power, 2, 1) + pltpu.roll(power, WIDE - 2, 1)) * 0.2
    floor_level = (water_level / (SEG_LEN + 1)) * jnp.sum(power, axis=1, keepdims=True)
    inverse_norm = lax.rsqrt(jnp.maximum(smooth, floor_level) + epsilon)
    return real_part * inverse_norm, imag_part * inverse_norm


def kernel(
    strain, channels, band, table, out,
    raw_high, raw_low, traces, pick, first, second, sources,
    trace_parts, spec, src_rows, src_spec, cross, table_v,
    table_sem, ag_send, ag_recv, p1_send, p1_recv, p2_send, p2_recv, p3_send, p3_recv,
):
    chan = lax.axis_index("chan")
    seg = lax.axis_index("seg")
    z, yh = chan // NYH, chan % NYH
    x, yl, core = seg // 4, (seg // 2) % 2, seg % 2
    half = seg // 2

    def at(chan_index, seg_index):
        return (chan_index, seg_index)

    def seg_of(x_, yl_, core_):
        return (x_ * 2 + yl_) * 2 + core_

    y_peer = at(chan, seg_of(x, 1 - yl, core))
    core_peer = at(chan, seg_of(x, yl, 1 - core))
    self_exchange = lax.rem(2 * half, NZ) == z

    barrier = pltpu.get_barrier_semaphore()

    def greet(device):
        pl.semaphore_signal(barrier, inc=1, device_id=device, device_id_type=MESH)

    greet(y_peer)
    greet(core_peer)
    for d in range(1, NX):
        greet(at(chan, seg_of(lax.rem(x + d, NX), yl, core)))
    for d in range(1, NYH):
        greet(at(z * NYH + lax.rem(yh + d, NYH), seg))
    for d in range(1, NZ):
        greet(at(lax.rem(z + d, NZ) * NYH + yh, seg))
    q = lax.rem(z - half + NZ, NZ)

    def greet_first(i, carry):
        zs, gs = i // 2, 2 * q + i % 2

        @pl.when(jnp.logical_not((zs == z) & (gs == seg)))
        def _():
            greet(at(zs * NYH + yh, gs))

        return carry

    lax.fori_loop(0, 16, greet_first, 0)

    table_copies = []
    for i, part in enumerate((0, 0, 1)):
        copy = pltpu.make_async_copy(
            table.at[part], table_v.at[WIDE * i : WIDE * i + WIDE], table_sem.at[i]
        )
        copy.start()
        table_copies.append(copy)

    for ref, part in ((raw_high, 0), (raw_low, 1)):
        ref[:, 0:128] = jnp.zeros((ROWS, 128), bf16)
        ref[:, 2560:2688] = jnp.zeros((ROWS, 128), bf16)
    body = split(strain[:, 0:2432])
    tail = split(strain[:, 2432:RAW])
    raw_high[:, 128:2560] = body[0]
    raw_low[:, 128:2560] = body[1]
    raw_high[:, 2560 : 2560 + 68] = tail[0]
    raw_low[:, 2560 : 2560 + 68] = tail[1]
    win_high = jnp.concatenate([raw_high[:, 512 * b : 512 * b + WIDE] for b in range(5)], axis=0)
    win_low = jnp.concatenate([raw_low[:, 512 * b : 512 * b + WIDE] for b in range(5)], axis=0)
    both = dot(jnp.concatenate([win_high, win_low], axis=0), band[0])
    dec = both[0:160] + both[160:320] + dot(win_high, band[1])
    dec = jnp.concatenate([dec[32 * b : 32 * b + 32] for b in range(5)], axis=1)
    traces[seg] = dec

    local = channels[...] - chan * ROWS
    onehot_t = (lax.broadcasted_iota(jnp.int32, (ROWS, SOURCES), 0) == local).astype(f32)
    picked = lax.dot_general(
        onehot_t, dec, (((0,), (0,)), ((), ())),
        precision=lax.Precision.HIGHEST, preferred_element_type=f32,
    )
    for j in range(SEGS):
        pick[j] = picked[2 * j : 2 * j + 2]

    @pl.when(self_exchange)
    def _():
        pl.semaphore_wait(barrier, 2 + 3 + 3 + 7 + 15)

    @pl.when(jnp.logical_not(self_exchange))
    def _():
        pl.semaphore_wait(barrier, 2 + 3 + 3 + 7 + 16)

    def first_copy(j):
        zd = lax.rem(half + j // 2, NZ)
        slot = z * 2 + core
        return pltpu.make_async_remote_copy(
            src_ref=pick.at[j], dst_ref=first.at[slot],
            send_sem=p1_send.at[j], recv_sem=p1_recv.at[slot],
            device_id=at(zd * NYH + yh, j), device_id_type=MESH,
        )

    def is_self(j):
        return self_exchange & (j == seg)

    def send_first(i, carry):
        j = lax.rem(seg + i, SEGS)

        @pl.when(jnp.logical_not(is_self(j)))
        def _():
            first_copy(j).start()

        return carry

    lax.fori_loop(0, SEGS, send_first, 0)

    @pl.when(self_exchange)
    def _():
        first[z * 2 + core] = pick[seg]

    started = []

    def begin(copy):
        copy.start()
        started.append(copy)

    def ag_copy(slot, index, device):
        return pltpu.make_async_remote_copy(
            src_ref=traces.at[slot], dst_ref=traces.at[slot],
            send_sem=ag_send.at[index], recv_sem=ag_recv.at[slot],
            device_id=device, device_id_type=MESH,
        )

    def ag_half(slot, part, index, device):
        rows = pl.ds(16 * part, 16)
        recv = ag_recv.at[slot] if part == 0 else ag_recv.at[SEGS]
        return pltpu.make_async_remote_copy(
            src_ref=traces.at[slot, rows], dst_ref=traces.at[slot, rows],
            send_sem=ag_send.at[index], recv_sem=recv,
            device_id=device, device_id_type=MESH,
        )

    def ag_wait(slot):
        ag_copy(slot, 0, core_peer).wait_recv()

    def near(d, other):
        return seg_of(lax.rem(x + d, NX), (1 - yl) if other else yl, core)

    x_next, x_last = at(chan, near(1, 0)), at(chan, near(3, 0))

    def ag_begin():
        begin(ag_copy(seg, 0, y_peer))
        begin(ag_copy(seg, 1, x_next))
        begin(ag_copy(seg, 2, x_last))
        begin(ag_copy(seg, 3, core_peer))

    def ag_relay_near():
        slot = near(0, 1)
        ag_wait(slot)
        begin(ag_copy(slot, 4, x_next))
        begin(ag_copy(slot, 5, x_last))
        begin(ag_copy(slot, 6, core_peer))
        slot = near(3, 0)
        ag_wait(slot)
        begin(ag_half(slot, 0, 7, x_next))
        begin(ag_copy(slot, 8, core_peer))
        slot = near(1, 0)
        ag_wait(slot)
        begin(ag_half(slot, 1, 9, x_last))
        begin(ag_copy(slot, 10, core_peer))

    def ag_relay_far():
        slot = near(2, 0)
        ag_half(slot, 0, 0, core_peer).wait_recv()
        ag_half(slot, 1, 0, core_peer).wait_recv()
        begin(ag_copy(slot, 11, y_peer))
        begin(ag_copy(slot, 12, core_peer))
        for index, slot in ((13, near(3, 1)), (14, near(1, 1)), (15, near(2, 1))):
            ag_wait(slot)
            begin(ag_copy(slot, index, core_peer))

    ag_begin()
    ag_relay_near()

    def wait_first(i, carry):
        zs, gs = i // 2, 2 * q + i % 2

        @pl.when(jnp.logical_not((zs == z) & (gs == seg)))
        def _():
            pltpu.make_async_remote_copy(
                src_ref=pick.at[0], dst_ref=first.at[i],
                send_sem=p1_send.at[0], recv_sem=p1_recv.at[i],
                device_id=core_peer, device_id_type=MESH,
            ).wait_recv()

        return carry

    lax.fori_loop(0, 16, wait_first, 0)
    for low in range(2):
        total = first[low]
        for zs in range(1, NZ):
            total = total + first[2 * zs + low]
        second[yh, low] = total

    def second_copy(d):
        return pltpu.make_async_remote_copy(
            src_ref=second.at[yh], dst_ref=second.at[yh],
            send_sem=p2_send.at[d], recv_sem=p2_recv.at[yh],
            device_id=at(z * NYH + lax.rem(yh + d, NYH), seg), device_id_type=MESH,
        )

    for d in (2, 1, 3):
        copy = second_copy(d)
        copy.start()
        started.append(copy)

    ag_relay_far()

    for d in range(1, NYH):
        slot = lax.rem(yh + d, NYH)
        pltpu.make_async_remote_copy(
            src_ref=second.at[slot], dst_ref=second.at[slot],
            send_sem=p2_send.at[d], recv_sem=p2_recv.at[slot],
            device_id=core_peer, device_id_type=MESH,
        ).wait_recv()
    for low in range(2):
        sources[q, low] = second[0, low] + second[1, low] + second[2, low] + second[3, low]

    def third_copy(slot, index, device):
        return pltpu.make_async_remote_copy(
            src_ref=sources.at[slot], dst_ref=sources.at[slot],
            send_sem=p3_send.at[index], recv_sem=p3_recv.at[slot],
            device_id=device, device_id_type=MESH,
        )

    for d in (4, 3, 5, 2, 6, 1, 7):
        copy = third_copy(q, d, at(lax.rem(z + d, NZ) * NYH + yh, seg))
        copy.start()
        started.append(copy)

    for x_ in range(NX):
        for yl_ in range(2):
            ag_wait(seg_of(x_, yl_, 1 - core))

    for copy in table_copies:
        copy.wait()

    lane = lax.broadcasted_iota(jnp.int32, (ROWS, 128), 1)

    def prepare(g, carry):
        before = jnp.maximum(g - 1, 0)
        spill = pltpu.roll(traces[before, :, 512:640], 15, 1)
        head = traces[g, :, 0:128] + jnp.where((lane < 15) & (g > 0), spill, 0.0)
        rows = pl.ds(pl.multiple_of(g * ROWS, ROWS), ROWS)
        for high, low, first_col, last_col in (
            (*split(head), 0, 128),
            (*split(traces[g, :, 128:640]), 128, 640),
        ):
            trace_parts[rows, first_col:last_col] = high
            trace_parts[rows, WIDE + first_col : WIDE + last_col] = low
            trace_parts[rows, 2 * WIDE + first_col : 2 * WIDE + last_col] = high
        return carry

    lax.fori_loop(0, SEGS, prepare, 0)

    def transform(block, carry):
        rows = pl.ds(pl.multiple_of((block // 5) * 256, 256), 256)
        cols = pl.ds(pl.multiple_of((block % 5) * 256, 256), 256)
        spec[rows, cols] = dot(trace_parts[rows, :], table_v[:, cols])
        return carry

    lax.fori_loop(0, 10, transform, 0)

    def whiten_rows(g, carry):
        rows = pl.ds(pl.multiple_of(g * 128, 128), 128)
        re, im = whiten(spec[rows, 0:640], spec[rows, 640:1280])
        spec[rows, 0:640] = re
        spec[rows, 640:1280] = im
        return carry

    lax.fori_loop(0, 4, whiten_rows, 0)

    for d in range(1, NZ):
        slot = lax.rem(q + d, NZ)
        third_copy(slot, 0, core_peer).wait_recv()
    for g in range(SEGS):
        for e in range(2):
            src_rows[e * 16 + g : e * 16 + g + 1, :] = sources[g // 2, g % 2, e : e + 1, :]
    lane16 = lax.broadcasted_iota(jnp.int32, (16, 128), 1)
    row16 = lax.broadcasted_iota(jnp.int32, (16, 128), 0)
    heads = []
    for e in range(2):
        spill = pltpu.roll(pltpu.roll(src_rows[e * 16 : e * 16 + 16, 512:640], 15, 1), 1, 0)
        keep = (lane16 < 15) & (row16 > 0)
        heads.append(src_rows[e * 16 : e * 16 + 16, 0:128] + jnp.where(keep, spill, 0.0))
    whole = jnp.concatenate([jnp.concatenate(heads, axis=0), src_rows[:, 128:640]], axis=1)
    s_high, s_low = split(whole)
    s_both = jnp.concatenate([s_high, s_low], axis=0)

    def transform_src(block, carry):
        cols = pl.ds(pl.multiple_of(block * 256, 256), 256)
        pair = dot(s_both, table_v[0:WIDE, cols])
        src_spec[:, cols] = pair[0:32] + pair[32:64] + dot(s_high, table_v[2 * WIDE : 3 * WIDE, cols])
        return carry

    lax.fori_loop(0, 5, transform_src, 0)
    re, im = whiten(src_spec[:, 0:640], src_spec[:, 640:1280])
    src_spec[:, 0:640] = re
    src_spec[:, 640:1280] = im

    factor = 1.0 / math.sqrt(2.0 * SEG_LEN * SEGS)

    def cross_block(block, carry):
        re_cols = pl.ds(pl.multiple_of(block * 128, 128), 128)
        im_cols = pl.ds(pl.multiple_of(640 + block * 128, 128), 128)
        freq = block * 128 + lane
        weight = jnp.where((freq == 0) | (freq == SEG_LEN), factor, 2.0 * factor)
        acc = [[jnp.zeros((ROWS, 128), f32) for _ in range(2)] for _ in range(2)]
        for g in range(SEGS):
            c_re = spec[g * ROWS : g * ROWS + ROWS, re_cols]
            c_im = spec[g * ROWS : g * ROWS + ROWS, im_cols]
            for e in range(2):
                s_re = src_spec[e * 16 + g : e * 16 + g + 1, re_cols]
                s_im = src_spec[e * 16 + g : e * 16 + g + 1, im_cols]
                acc[e][0] = acc[e][0] + (s_re * c_re + s_im * c_im)
                acc[e][1] = acc[e][1] + (s_re * c_im - s_im * c_re)
        for e in range(2):
            cross[e * ROWS : e * ROWS + ROWS, re_cols] = acc[e][0] * weight
            cross[e * ROWS : e * ROWS + ROWS, im_cols] = acc[e][1] * weight
        return carry

    lax.fori_loop(0, 5, cross_block, 0)

    parts = []
    for base in (0, 640):
        c_high, c_low = split(cross[:, base : base + 640])
        pair = dot_t(jnp.concatenate([c_high, c_low], axis=0), table_v[0:256, base : base + 640])
        parts.append(
            pair[0:64] + pair[64:128] + dot_t(c_high, table_v[2 * WIDE : 2 * WIDE + 256, base : base + 640])
        )
    even, odd = parts
    lags = jnp.concatenate([even - odd, even + odd], axis=1)
    l_high, l_low = split(lags)
    l_last = (lags - l_high.astype(f32) - l_low.astype(f32)).astype(bf16)
    row = lax.broadcasted_iota(jnp.int32, (512, 512), 0)
    col = lax.broadcasted_iota(jnp.int32, (512, 512), 1)
    negative = (row > 0) & (row < 256) & (col == MAXLAG - row)
    positive = (row >= 256) & (col == MAXLAG - 256 + row)
    place = jnp.where(negative | positive, 1.0, 0.0).astype(bf16)
    moved = dot(jnp.concatenate([l_high, l_low, l_last], axis=0), place)
    placed = moved[0:64] + moved[64:128] + moved[128:192]
    for e in range(2):
        out[e] = placed[e * ROWS : e * ROWS + ROWS, 0 : 2 * MAXLAG + 1]

    for copy in started:
        copy.wait_send()

    def wait_send_first(j, carry):
        @pl.when(jnp.logical_not(is_self(j)))
        def _():
            first_copy(j).wait_send()

        return carry

    lax.fori_loop(0, SEGS, wait_send_first, 0)


def body(strain, source_channels):
    vmem = pl.BlockSpec(memory_space=pltpu.VMEM)
    sem = pltpu.SemaphoreType.DMA
    return pl.pallas_call(
        kernel,
        out_shape=jax.ShapeDtypeStruct((2, ROWS, 2 * MAXLAG + 1), f32),
        in_specs=[vmem, vmem, vmem, pl.BlockSpec(memory_space=pl.ANY)],
        out_specs=vmem,
        scratch_shapes=[
            pltpu.VMEM((ROWS, 2688), bf16),
            pltpu.VMEM((ROWS, 2688), bf16),
            pltpu.VMEM((SEGS, ROWS, WIDE), f32),
            pltpu.VMEM((SEGS, 2, WIDE), f32),
            pltpu.VMEM((16, 2, WIDE), f32),
            pltpu.VMEM((NYH, 2, 2, WIDE), f32),
            pltpu.VMEM((NZ, 2, 2, WIDE), f32),
            pltpu.VMEM((SEGS * ROWS, 3 * WIDE), bf16),
            pltpu.VMEM((SEGS * ROWS, 2 * WIDE), f32),
            pltpu.VMEM((32, WIDE), f32),
            pltpu.VMEM((32, 2 * WIDE), f32),
            pltpu.VMEM((64, 2 * WIDE), f32),
            pltpu.VMEM((3 * WIDE, 2 * WIDE), bf16),
            sem((3,)), sem((16,)), sem((17,)), sem((16,)), sem((16,)),
            sem((4,)), sem((4,)), sem((8,)), sem((8,)),
        ],
        compiler_params=pltpu.CompilerParams(collective_id=0, has_side_effects=True),
        name="noise_stack",
    )(strain, source_channels.reshape(1, SOURCES), jnp.asarray(band_table()), jnp.asarray(forward_table()))


def solution(mesh):
    in_specs = (P("chan", "seg"), P())
    out_specs = P("seg", "chan", None)
    return jax.shard_map(body, mesh=mesh, in_specs=in_specs, out_specs=out_specs, check_vma=False)
```

```python
import math

import jax
import jax.numpy as jnp
import ml_dtypes
import numpy as np
from jax import lax
from jax.experimental import pallas as pl
from jax.experimental.pallas import tpu as pltpu
from jax.sharding import PartitionSpec as P

SEG_LEN = 625
TAPS = 63
MAXLAG = 250
SEGS = 16
SOURCES = 32
ROWS = 32
WIDE = 640
RAW = 2500
NZ, NYH, NX = 8, 4, 4

cutoff = 0.1
water_level = 0.5
epsilon = 1e-06

MESH = pl.DeviceIdType.MESH
f32 = jnp.float32
bf16 = jnp.bfloat16


def split_table(table):
    high = table.astype(np.float32).astype(ml_dtypes.bfloat16)
    low = (table - high.astype(np.float64)).astype(np.float32).astype(ml_dtypes.bfloat16)
    return np.stack([high, low])


def band_table():
    position = np.arange(TAPS, dtype=np.float64)
    window = 0.54 - 0.46 * np.cos(2.0 * math.pi * position / (TAPS - 1))
    taps = window * 2.0 * cutoff * np.sinc(2.0 * cutoff * (position - (TAPS - 1) / 2.0))
    taps = taps / taps.sum()
    index = 4 * np.arange(128)[None, :] + 130 - np.arange(WIDE)[:, None]
    valid = (index >= 0) & (index < TAPS)
    return split_table(np.where(valid, taps[np.clip(index, 0, TAPS - 1)], 0.0))


def forward_table():
    samples = np.arange(WIDE)[:, None]
    freqs = np.arange(WIDE)[None, :]
    phase = ((samples * freqs) % (2 * SEG_LEN)) * (math.pi / SEG_LEN)
    valid = (freqs <= SEG_LEN) & (samples < SEG_LEN)
    table = np.concatenate(
        [np.where(valid, np.cos(phase), 0.0), np.where(valid, -np.sin(phase), 0.0)], axis=1
    )
    return split_table(table)


def split(value):
    high = value.astype(bf16)
    return high, (value - high.astype(f32)).astype(bf16)


def dot(a, b):
    return jnp.dot(a, b, preferred_element_type=f32)


def dot_t(a, b):
    return lax.dot_general(a, b, (((1,), (1,)), ((), ())), preferred_element_type=f32)


def whiten(real_part, imag_part):
    power = real_part * real_part + imag_part * imag_part
    near = power + pltpu.roll(power, 1, 1) + pltpu.roll(power, WIDE - 1, 1)
    smooth = (near + pltpu.roll(power, 2, 1) + pltpu.roll(power, WIDE - 2, 1)) * 0.2
    floor_level = (water_level / (SEG_LEN + 1)) * jnp.sum(power, axis=1, keepdims=True)
    inverse_norm = lax.rsqrt(jnp.maximum(smooth, floor_level) + epsilon)
    return real_part * inverse_norm, imag_part * inverse_norm


def kernel(
    strain_in, channels_in, band_in, table, out,
    strain, channels, band, place, raw_high, raw_low, traces, pick, first, second, sources,
    trace_parts, spills, spill_table, spec, src_rows, src_last, src_spec, cross, table_v,
    table_sem, ag_send, ag_recv, p1_send, p1_recv, p2_send, p2_recv, p3_send, p3_recv,
):
    chan = lax.axis_index("chan")
    seg = lax.axis_index("seg")
    z, yh = chan // NYH, chan % NYH
    x, yl, core = seg // 4, (seg // 2) % 2, seg % 2
    half = seg // 2

    def at(chan_index, seg_index):
        return (chan_index, seg_index)

    def seg_of(x_, yl_, core_):
        return (x_ * 2 + yl_) * 2 + core_

    y_peer = at(chan, seg_of(x, 1 - yl, core))
    core_peer = at(chan, seg_of(x, yl, 1 - core))
    self_exchange = lax.rem(2 * half, NZ) == z

    barrier = pltpu.get_barrier_semaphore()

    def greet(device):
        pl.semaphore_signal(barrier, inc=1, device_id=device, device_id_type=MESH)

    greet(y_peer)
    greet(core_peer)
    for d in range(1, NX):
        greet(at(chan, seg_of(lax.rem(x + d, NX), yl, core)))
    for d in range(1, NYH):
        greet(at(z * NYH + lax.rem(yh + d, NYH), seg))
    for d in range(1, NZ):
        greet(at(lax.rem(z + d, NZ) * NYH + yh, seg))
    q = lax.rem(z - half + NZ, NZ)

    def greet_first(i, carry):
        zs, gs = i // 2, 2 * q + i % 2

        @pl.when(jnp.logical_not((zs == z) & (gs == seg)))
        def _():
            greet(at(zs * NYH + yh, gs))

        return carry

    lax.fori_loop(0, 16, greet_first, 0)

    inputs = []
    for i, (source, target) in enumerate(
        ((strain_in, strain), (band_in, band), (channels_in, channels))
    ):
        copy = pltpu.make_async_copy(source, target, table_sem.at[3 + i])
        copy.start()
        inputs.append(copy)
    table_copies = []
    for i, part in enumerate((0, 0, 1)):
        copy = pltpu.make_async_copy(
            table.at[part], table_v.at[WIDE * i : WIDE * i + WIDE], table_sem.at[i]
        )
        copy.start()
        table_copies.append(copy)

    for ref, part in ((raw_high, 0), (raw_low, 1)):
        ref[:, 0:128] = jnp.zeros((ROWS, 128), bf16)
        ref[:, 2560:2688] = jnp.zeros((ROWS, 128), bf16)
    for copy in inputs:
        copy.wait()
    body = split(strain[:, 0:2432])
    tail = split(strain[:, 2432:RAW])
    raw_high[:, 128:2560] = body[0]
    raw_low[:, 128:2560] = body[1]
    raw_high[:, 2560 : 2560 + 68] = tail[0]
    raw_low[:, 2560 : 2560 + 68] = tail[1]
    win_high = jnp.concatenate([raw_high[:, 512 * b : 512 * b + WIDE] for b in range(5)], axis=0)
    win_low = jnp.concatenate([raw_low[:, 512 * b : 512 * b + WIDE] for b in range(5)], axis=0)
    both = dot(jnp.concatenate([win_high, win_low], axis=0), band[0])
    dec = both[0:160] + both[160:320] + dot(win_high, band[1])
    dec = jnp.concatenate([dec[32 * b : 32 * b + 32] for b in range(5)], axis=1)
    traces[seg] = dec

    local = channels[...] - chan * ROWS
    onehot_t = (lax.broadcasted_iota(jnp.int32, (ROWS, SOURCES), 0) == local).astype(f32)
    picked = lax.dot_general(
        onehot_t, dec, (((0,), (0,)), ((), ())),
        precision=lax.Precision.HIGHEST, preferred_element_type=f32,
    )
    for j in range(SEGS):
        pick[j] = picked[2 * j : 2 * j + 2]

    @pl.when(self_exchange)
    def _():
        pl.semaphore_wait(barrier, 2 + 3 + 3 + 7 + 15)

    @pl.when(jnp.logical_not(self_exchange))
    def _():
        pl.semaphore_wait(barrier, 2 + 3 + 3 + 7 + 16)

    def first_copy(j):
        zd = lax.rem(half + j // 2, NZ)
        slot = z * 2 + core
        return pltpu.make_async_remote_copy(
            src_ref=pick.at[j], dst_ref=first.at[slot],
            send_sem=p1_send.at[j], recv_sem=p1_recv.at[slot],
            device_id=at(zd * NYH + yh, j), device_id_type=MESH,
        )

    def is_self(j):
        return self_exchange & (j == seg)

    def send_first(i, carry):
        j = lax.rem(seg + i, SEGS)

        @pl.when(jnp.logical_not(is_self(j)))
        def _():
            first_copy(j).start()

        return carry

    lax.fori_loop(0, SEGS, send_first, 0)

    @pl.when(self_exchange)
    def _():
        first[z * 2 + core] = pick[seg]

    started = []

    def begin(copy):
        copy.start()
        started.append(copy)

    def ag_copy(slot, index, device):
        return pltpu.make_async_remote_copy(
            src_ref=traces.at[slot], dst_ref=traces.at[slot],
            send_sem=ag_send.at[index], recv_sem=ag_recv.at[slot],
            device_id=device, device_id_type=MESH,
        )

    def ag_half(slot, part, index, device):
        rows = pl.ds(16 * part, 16)
        recv = ag_recv.at[slot] if part == 0 else ag_recv.at[SEGS]
        return pltpu.make_async_remote_copy(
            src_ref=traces.at[slot, rows], dst_ref=traces.at[slot, rows],
            send_sem=ag_send.at[index], recv_sem=recv,
            device_id=device, device_id_type=MESH,
        )

    def ag_wait(slot):
        ag_copy(slot, 0, core_peer).wait_recv()

    def near(d, other):
        return seg_of(lax.rem(x + d, NX), (1 - yl) if other else yl, core)

    x_next, x_last = at(chan, near(1, 0)), at(chan, near(3, 0))

    def ag_begin():
        begin(ag_copy(seg, 0, y_peer))
        begin(ag_copy(seg, 1, x_next))
        begin(ag_copy(seg, 2, x_last))
        begin(ag_copy(seg, 3, core_peer))

    def ag_relay_near():
        slot = near(0, 1)
        ag_wait(slot)
        begin(ag_copy(slot, 4, x_next))
        begin(ag_copy(slot, 5, x_last))
        begin(ag_copy(slot, 6, core_peer))
        slot = near(3, 0)
        ag_wait(slot)
        begin(ag_half(slot, 0, 7, x_next))
        begin(ag_copy(slot, 8, core_peer))
        slot = near(1, 0)
        ag_wait(slot)
        begin(ag_half(slot, 1, 9, x_last))
        begin(ag_copy(slot, 10, core_peer))

    def ag_relay_far():
        slot = near(2, 0)
        ag_half(slot, 0, 0, core_peer).wait_recv()
        ag_half(slot, 1, 0, core_peer).wait_recv()
        begin(ag_copy(slot, 11, y_peer))
        begin(ag_copy(slot, 12, core_peer))
        for index, slot in ((13, near(3, 1)), (14, near(1, 1)), (15, near(2, 1))):
            ag_wait(slot)
            begin(ag_copy(slot, index, core_peer))

    lane = lax.broadcasted_iota(jnp.int32, (ROWS, 128), 1)

    def slot_of(place_index):
        group, i = place_index // 4, place_index % 4
        far, twin = group // 2, group % 2
        d_near = jnp.where(i < 2, 0, jnp.where(i == 2, 3, 1))
        d_far = jnp.where(i < 2, 2, jnp.where(i == 2, 3, 1))
        other_near = jnp.where(i == 1, 1, 0)
        other_far = jnp.where(i == 0, 0, 1)
        d = jnp.where(far == 1, d_far, d_near)
        other = jnp.where(far == 1, other_far, other_near)
        return (lax.rem(x + d, NX) * 2 + lax.rem(yl + other, 2)) * 2 + lax.rem(core + twin, 2)

    def rows_of(place_index):
        return pl.ds(pl.multiple_of(place_index * ROWS, ROWS), ROWS)

    def store_parts(place_index, first_col, last_col, value):
        rows = rows_of(place_index)
        high, low = split(value)
        trace_parts[rows, first_col:last_col] = high
        trace_parts[rows, WIDE + first_col : WIDE + last_col] = low
        trace_parts[rows, 2 * WIDE + first_col : 2 * WIDE + last_col] = high

    def prepare_four(group):
        def prepare(i, carry):
            store_parts(i, 0, 640, traces[slot_of(i)])
            return carry

        lax.fori_loop(4 * group, 4 * group + 4, prepare, 0)

    def transform(rows, first_row):
        def block(i, carry):
            at_rows = pl.ds(first_row, rows)
            cols = pl.ds(pl.multiple_of(i * 256, 256), 256)
            spec[at_rows, cols] = dot(trace_parts[at_rows, :], table_v[:, cols])
            return carry

        lax.fori_loop(0, 5, block, 0)

    def partner(d, other):
        return seg_of(lax.rem(x + d, NX), (1 - yl) if other else yl, 1 - core)

    ag_begin()
    ag_relay_near()
    prepare_four(0)
    for copy in table_copies:
        copy.wait()
    spill_table[...] = jnp.zeros((128, 2 * WIDE), bf16)
    spill_table[0:16, :] = table_v[0:16, :]
    spill_table[16:32, :] = table_v[0:16, :]
    spill_table[32:48, :] = table_v[2 * WIDE : 2 * WIDE + 16, :]
    transform(128, 0)

    row = lax.broadcasted_iota(jnp.int32, (512, 512), 0)
    col = lax.broadcasted_iota(jnp.int32, (512, 512), 1)
    negative = (row > 0) & (row < 256) & (col == MAXLAG - row)
    positive = (row >= 256) & (col == MAXLAG - 256 + row)
    place[...] = jnp.where(negative | positive, 1.0, 0.0).astype(bf16)

    def wait_first(i, carry):
        zs, gs = i // 2, 2 * q + i % 2

        @pl.when(jnp.logical_not((zs == z) & (gs == seg)))
        def _():
            pltpu.make_async_remote_copy(
                src_ref=pick.at[0], dst_ref=first.at[i],
                send_sem=p1_send.at[0], recv_sem=p1_recv.at[i],
                device_id=core_peer, device_id_type=MESH,
            ).wait_recv()

        return carry

    lax.fori_loop(0, 16, wait_first, 0)
    for low in range(2):
        total = first[low]
        for zs in range(1, NZ):
            total = total + first[2 * zs + low]
        second[yh, low] = total

    def second_copy(d):
        return pltpu.make_async_remote_copy(
            src_ref=second.at[yh], dst_ref=second.at[yh],
            send_sem=p2_send.at[d], recv_sem=p2_recv.at[yh],
            device_id=at(z * NYH + lax.rem(yh + d, NYH), seg), device_id_type=MESH,
        )

    for d in (2, 1, 3):
        copy = second_copy(d)
        copy.start()
        started.append(copy)

    for d, other in ((0, 0), (0, 1), (3, 0), (1, 0)):
        ag_wait(partner(d, other))
    prepare_four(1)
    transform(128, 128)
    ag_relay_far()
    prepare_four(2)

    for d in range(1, NYH):
        slot = lax.rem(yh + d, NYH)
        pltpu.make_async_remote_copy(
            src_ref=second.at[slot], dst_ref=second.at[slot],
            send_sem=p2_send.at[d], recv_sem=p2_recv.at[slot],
            device_id=core_peer, device_id_type=MESH,
        ).wait_recv()
    for low in range(2):
        sources[q, low] = second[0, low] + second[1, low] + second[2, low] + second[3, low]

    def third_copy(slot, index, device):
        return pltpu.make_async_remote_copy(
            src_ref=sources.at[slot], dst_ref=sources.at[slot],
            send_sem=p3_send.at[index], recv_sem=p3_recv.at[slot],
            device_id=device, device_id_type=MESH,
        )

    for d in (4, 3, 5, 2, 6, 1, 7):
        copy = third_copy(q, d, at(lax.rem(z + d, NZ) * NYH + yh, seg))
        copy.start()
        started.append(copy)

    for d, other in ((2, 0), (2, 1), (3, 1), (1, 1)):
        ag_wait(partner(d, other))
    prepare_four(3)

    def place_spill(i, carry):
        g = slot_of(i)
        last = traces[jnp.maximum(g - 1, 0), :, 512:640]
        high, low = split(jnp.where(g > 0, last, 0.0))
        high, low = high.astype(f32), low.astype(f32)
        parts = jnp.where(lane < 15, pltpu.roll(high, 15, 1), 0.0)
        parts = jnp.where((lane >= 16) & (lane < 31), pltpu.roll(low, 31, 1), parts)
        parts = jnp.where((lane >= 32) & (lane < 47), pltpu.roll(high, 47, 1), parts)
        spills[rows_of(i), :] = parts.astype(bf16)
        return carry

    lax.fori_loop(0, SEGS, place_spill, 0)
    transform(256, 256)

    def whiten_rows(g, carry):
        rows = pl.ds(pl.multiple_of(g * 128, 128), 128)
        early = dot(spills[rows, :], spill_table[...])
        re, im = whiten(
            spec[rows, 0:640] + early[:, 0:640], spec[rows, 640:1280] + early[:, 640:1280]
        )
        spec[rows, 0:640] = re
        spec[rows, 640:1280] = im
        return carry

    lax.fori_loop(0, 4, whiten_rows, 0)

    for d in range(1, NZ):
        slot = lax.rem(q + d, NZ)
        third_copy(slot, 0, core_peer).wait_recv()
    for p in range(SEGS):
        g = slot_of(p)
        prev = jnp.maximum(g - 1, 0)
        for e in range(2):
            row = e * 16 + p
            src_rows[row : row + 1, :] = sources[g // 2, g % 2, e : e + 1, :]
            last = sources[prev // 2, prev % 2, e : e + 1, 512:640]
            src_last[row : row + 1, :] = jnp.where(g > 0, last, 0.0)
    spill = jnp.where(lane < 15, pltpu.roll(src_last[...], 15, 1), 0.0)
    whole = jnp.concatenate([src_rows[:, 0:128] + spill, src_rows[:, 128:640]], axis=1)
    s_high, s_low = split(whole)
    s_both = jnp.concatenate([s_high, s_low], axis=0)

    def transform_src(block, carry):
        cols = pl.ds(pl.multiple_of(block * 256, 256), 256)
        pair = dot(s_both, table_v[0:WIDE, cols])
        src_spec[:, cols] = pair[0:32] + pair[32:64] + dot(s_high, table_v[2 * WIDE : 3 * WIDE, cols])
        return carry

    lax.fori_loop(0, 5, transform_src, 0)
    re, im = whiten(src_spec[:, 0:640], src_spec[:, 640:1280])
    src_spec[:, 0:640] = re
    src_spec[:, 640:1280] = im

    factor = 1.0 / math.sqrt(2.0 * SEG_LEN * SEGS)

    def cross_block(block, carry):
        re_cols = pl.ds(pl.multiple_of(block * 128, 128), 128)
        im_cols = pl.ds(pl.multiple_of(640 + block * 128, 128), 128)
        freq = block * 128 + lane
        weight = jnp.where((freq == 0) | (freq == SEG_LEN), factor, 2.0 * factor)
        acc = [[jnp.zeros((ROWS, 128), f32) for _ in range(2)] for _ in range(2)]
        for g in range(SEGS):
            c_re = spec[g * ROWS : g * ROWS + ROWS, re_cols]
            c_im = spec[g * ROWS : g * ROWS + ROWS, im_cols]
            for e in range(2):
                s_re = src_spec[e * 16 + g : e * 16 + g + 1, re_cols]
                s_im = src_spec[e * 16 + g : e * 16 + g + 1, im_cols]
                acc[e][0] = acc[e][0] + (s_re * c_re + s_im * c_im)
                acc[e][1] = acc[e][1] + (s_re * c_im - s_im * c_re)
        for e in range(2):
            cross[e * ROWS : e * ROWS + ROWS, re_cols] = acc[e][0] * weight
            cross[e * ROWS : e * ROWS + ROWS, im_cols] = acc[e][1] * weight
        return carry

    lax.fori_loop(0, 5, cross_block, 0)

    parts = []
    for base in (0, 640):
        c_high, c_low = split(cross[:, base : base + 640])
        pair = dot_t(jnp.concatenate([c_high, c_low], axis=0), table_v[0:256, base : base + 640])
        parts.append(
            pair[0:64] + pair[64:128] + dot_t(c_high, table_v[2 * WIDE : 2 * WIDE + 256, base : base + 640])
        )
    even, odd = parts
    lags = jnp.concatenate([even - odd, even + odd], axis=1)
    l_high, l_low = split(lags)
    l_last = (lags - l_high.astype(f32) - l_low.astype(f32)).astype(bf16)
    moved = dot(jnp.concatenate([l_high, l_low, l_last], axis=0), place[...])
    placed = moved[0:64] + moved[64:128] + moved[128:192]
    for e in range(2):
        out[e] = placed[e * ROWS : e * ROWS + ROWS, 0 : 2 * MAXLAG + 1]

    for copy in started:
        copy.wait_send()

    def wait_send_first(j, carry):
        @pl.when(jnp.logical_not(is_self(j)))
        def _():
            first_copy(j).wait_send()

        return carry

    lax.fori_loop(0, SEGS, wait_send_first, 0)


def body(strain, source_channels):
    vmem = pl.BlockSpec(memory_space=pltpu.VMEM)
    sem = pltpu.SemaphoreType.DMA
    return pl.pallas_call(
        kernel,
        out_shape=jax.ShapeDtypeStruct((2, ROWS, 2 * MAXLAG + 1), f32),
        in_specs=[pl.BlockSpec(memory_space=pl.ANY)] * 4,
        out_specs=vmem,
        scratch_shapes=[
            pltpu.VMEM((ROWS, RAW), f32),
            pltpu.VMEM((1, SOURCES), jnp.int32),
            pltpu.VMEM((2, WIDE, 128), bf16),
            pltpu.VMEM((512, 512), bf16),
            pltpu.VMEM((ROWS, 2688), bf16),
            pltpu.VMEM((ROWS, 2688), bf16),
            pltpu.VMEM((SEGS, ROWS, WIDE), f32),
            pltpu.VMEM((SEGS, 2, WIDE), f32),
            pltpu.VMEM((16, 2, WIDE), f32),
            pltpu.VMEM((NYH, 2, 2, WIDE), f32),
            pltpu.VMEM((NZ, 2, 2, WIDE), f32),
            pltpu.VMEM((SEGS * ROWS, 3 * WIDE), bf16),
            pltpu.VMEM((SEGS * ROWS, 128), bf16),
            pltpu.VMEM((128, 2 * WIDE), bf16),
            pltpu.VMEM((SEGS * ROWS, 2 * WIDE), f32),
            pltpu.VMEM((32, WIDE), f32),
            pltpu.VMEM((32, 128), f32),
            pltpu.VMEM((32, 2 * WIDE), f32),
            pltpu.VMEM((64, 2 * WIDE), f32),
            pltpu.VMEM((3 * WIDE, 2 * WIDE), bf16),
            sem((6,)), sem((16,)), sem((17,)), sem((16,)), sem((16,)),
            sem((4,)), sem((4,)), sem((8,)), sem((8,)),
        ],
        compiler_params=pltpu.CompilerParams(collective_id=0, has_side_effects=True),
        name="noise_stack",
    )(strain, source_channels.reshape(1, SOURCES), jnp.asarray(band_table()), jnp.asarray(forward_table()))


def solution(mesh):
    in_specs = (P("chan", "seg"), P())
    out_specs = P("seg", "chan", None)
    return jax.shard_map(body, mesh=mesh, in_specs=in_specs, out_specs=out_specs, check_vma=False)
```

```python
import math

import jax
import jax.numpy as jnp
import ml_dtypes
import numpy as np
from jax import lax
from jax.experimental import pallas as pl
from jax.experimental.pallas import tpu as pltpu
from jax.sharding import PartitionSpec as P

SEG_LEN = 625
TAPS = 63
MAXLAG = 250
SEGS = 16
SOURCES = 32
ROWS = 32
WIDE = 640
RAW = 2500
NZ, NYH, NX = 8, 4, 4

cutoff = 0.1
water_level = 0.5
epsilon = 1e-06

MESH = pl.DeviceIdType.MESH
f32 = jnp.float32
bf16 = jnp.bfloat16


def split_table(table):
    high = table.astype(np.float32).astype(ml_dtypes.bfloat16)
    low = (table - high.astype(np.float64)).astype(np.float32).astype(ml_dtypes.bfloat16)
    return np.stack([high, low])


def band_table():
    position = np.arange(TAPS, dtype=np.float64)
    window = 0.54 - 0.46 * np.cos(2.0 * math.pi * position / (TAPS - 1))
    taps = window * 2.0 * cutoff * np.sinc(2.0 * cutoff * (position - (TAPS - 1) / 2.0))
    taps = taps / taps.sum()
    index = 4 * np.arange(128)[None, :] + 130 - np.arange(WIDE)[:, None]
    valid = (index >= 0) & (index < TAPS)
    return split_table(np.where(valid, taps[np.clip(index, 0, TAPS - 1)], 0.0))


def forward_table():
    samples = np.arange(WIDE)[:, None]
    freqs = np.arange(WIDE)[None, :]
    phase = ((samples * freqs) % (2 * SEG_LEN)) * (math.pi / SEG_LEN)
    valid = (freqs <= SEG_LEN) & (samples < SEG_LEN)
    table = np.concatenate(
        [np.where(valid, np.cos(phase), 0.0), np.where(valid, -np.sin(phase), 0.0)], axis=1
    )
    return split_table(table)


def split(value):
    high = value.astype(bf16)
    return high, (value - high.astype(f32)).astype(bf16)


def dot(a, b):
    return jnp.dot(a, b, preferred_element_type=f32)


def dot_t(a, b):
    return lax.dot_general(a, b, (((1,), (1,)), ((), ())), preferred_element_type=f32)


def whiten(real_part, imag_part):
    power = real_part * real_part + imag_part * imag_part
    near = power + pltpu.roll(power, 1, 1) + pltpu.roll(power, WIDE - 1, 1)
    smooth = (near + pltpu.roll(power, 2, 1) + pltpu.roll(power, WIDE - 2, 1)) * 0.2
    floor_level = (water_level / (SEG_LEN + 1)) * jnp.sum(power, axis=1, keepdims=True)
    inverse_norm = lax.rsqrt(jnp.maximum(smooth, floor_level) + epsilon)
    return real_part * inverse_norm, imag_part * inverse_norm


def kernel(
    strain_in, channels_in, band_in, table, out,
    strain, channels, band, place, raw_high, raw_low, traces, pick, first, second, sources,
    trace_parts, spills, spill_table, spec, src_rows, src_last, src_spec, cross, table_v,
    table_sem, ag_send, ag_recv, p1_send, p1_recv, p2_send, p2_recv, p3_send, p3_recv,
):
    chan = lax.axis_index("chan")
    seg = lax.axis_index("seg")
    z, yh = chan // NYH, chan % NYH
    x, yl, core = seg // 4, (seg // 2) % 2, seg % 2
    half = seg // 2

    def at(chan_index, seg_index):
        return (chan_index, seg_index)

    def seg_of(x_, yl_, core_):
        return (x_ * 2 + yl_) * 2 + core_

    y_peer = at(chan, seg_of(x, 1 - yl, core))
    core_peer = at(chan, seg_of(x, yl, 1 - core))
    self_exchange = lax.rem(2 * half, NZ) == z

    inputs = []
    for i, (source, target) in enumerate(
        ((strain_in, strain), (band_in, band), (channels_in, channels))
    ):
        copy = pltpu.make_async_copy(source, target, table_sem.at[3 + i])
        copy.start()
        inputs.append(copy)

    barrier = pltpu.get_barrier_semaphore()

    def greet(device):
        pl.semaphore_signal(barrier, inc=1, device_id=device, device_id_type=MESH)

    greet(y_peer)
    greet(core_peer)
    for d in range(1, NX):
        greet(at(chan, seg_of(lax.rem(x + d, NX), yl, core)))
    for d in range(1, NYH):
        greet(at(z * NYH + lax.rem(yh + d, NYH), seg))
    for d in range(1, NZ):
        greet(at(lax.rem(z + d, NZ) * NYH + yh, seg))
    q = lax.rem(z - half + NZ, NZ)

    def greet_first(i, carry):
        zs, gs = i // 2, 2 * q + i % 2

        @pl.when(jnp.logical_not((zs == z) & (gs == seg)))
        def _():
            greet(at(zs * NYH + yh, gs))

        return carry

    lax.fori_loop(0, 16, greet_first, 0)

    table_copies = []
    for i, part in enumerate((0, 0, 1)):
        copy = pltpu.make_async_copy(
            table.at[part], table_v.at[WIDE * i : WIDE * i + WIDE], table_sem.at[i]
        )
        copy.start()
        table_copies.append(copy)

    for ref, part in ((raw_high, 0), (raw_low, 1)):
        ref[:, 0:128] = jnp.zeros((ROWS, 128), bf16)
        ref[:, 2560:2688] = jnp.zeros((ROWS, 128), bf16)
    for copy in inputs:
        copy.wait()
    body = split(strain[:, 0:2432])
    tail = split(strain[:, 2432:RAW])
    raw_high[:, 128:2560] = body[0]
    raw_low[:, 128:2560] = body[1]
    raw_high[:, 2560 : 2560 + 68] = tail[0]
    raw_low[:, 2560 : 2560 + 68] = tail[1]
    win_high = jnp.concatenate([raw_high[:, 512 * b : 512 * b + WIDE] for b in range(5)], axis=0)
    win_low = jnp.concatenate([raw_low[:, 512 * b : 512 * b + WIDE] for b in range(5)], axis=0)
    both = dot(jnp.concatenate([win_high, win_low], axis=0), band[0])
    dec = both[0:160] + both[160:320] + dot(win_high, band[1])
    dec = jnp.concatenate([dec[32 * b : 32 * b + 32] for b in range(5)], axis=1)
    traces[seg] = dec

    local = channels[...] - chan * ROWS
    onehot_t = (lax.broadcasted_iota(jnp.int32, (ROWS, SOURCES), 0) == local).astype(f32)
    picked = lax.dot_general(
        onehot_t, dec, (((0,), (0,)), ((), ())),
        precision=lax.Precision.HIGHEST, preferred_element_type=f32,
    )
    for j in range(SEGS):
        pick[j] = picked[2 * j : 2 * j + 2]

    @pl.when(self_exchange)
    def _():
        pl.semaphore_wait(barrier, 2 + 3 + 3 + 7 + 15)

    @pl.when(jnp.logical_not(self_exchange))
    def _():
        pl.semaphore_wait(barrier, 2 + 3 + 3 + 7 + 16)

    def first_copy(j):
        zd = lax.rem(half + j // 2, NZ)
        slot = z * 2 + core
        return pltpu.make_async_remote_copy(
            src_ref=pick.at[j], dst_ref=first.at[slot],
            send_sem=p1_send.at[j], recv_sem=p1_recv.at[slot],
            device_id=at(zd * NYH + yh, j), device_id_type=MESH,
        )

    def is_self(j):
        return self_exchange & (j == seg)

    def send_first(i, carry):
        j = lax.rem(seg + i, SEGS)

        @pl.when(jnp.logical_not(is_self(j)))
        def _():
            first_copy(j).start()

        return carry

    lax.fori_loop(0, SEGS, send_first, 0)

    @pl.when(self_exchange)
    def _():
        first[z * 2 + core] = pick[seg]

    started = []

    def begin(copy):
        copy.start()
        started.append(copy)

    def ag_copy(slot, index, device):
        return pltpu.make_async_remote_copy(
            src_ref=traces.at[slot], dst_ref=traces.at[slot],
            send_sem=ag_send.at[index], recv_sem=ag_recv.at[slot],
            device_id=device, device_id_type=MESH,
        )

    def ag_half(slot, part, index, device):
        rows = pl.ds(16 * part, 16)
        recv = ag_recv.at[slot] if part == 0 else ag_recv.at[SEGS]
        return pltpu.make_async_remote_copy(
            src_ref=traces.at[slot, rows], dst_ref=traces.at[slot, rows],
            send_sem=ag_send.at[index], recv_sem=recv,
            device_id=device, device_id_type=MESH,
        )

    def ag_wait(slot):
        ag_copy(slot, 0, core_peer).wait_recv()

    def near(d, other):
        return seg_of(lax.rem(x + d, NX), (1 - yl) if other else yl, core)

    x_next, x_last = at(chan, near(1, 0)), at(chan, near(3, 0))

    def ag_begin():
        begin(ag_copy(seg, 0, y_peer))
        begin(ag_copy(seg, 1, x_next))
        begin(ag_copy(seg, 2, x_last))
        begin(ag_copy(seg, 3, core_peer))

    def ag_relay_near():
        slot = near(0, 1)
        ag_wait(slot)
        begin(ag_copy(slot, 4, x_next))
        begin(ag_copy(slot, 5, x_last))
        begin(ag_copy(slot, 6, core_peer))
        slot = near(3, 0)
        ag_wait(slot)
        begin(ag_half(slot, 0, 7, x_next))
        begin(ag_copy(slot, 8, core_peer))
        slot = near(1, 0)
        ag_wait(slot)
        begin(ag_half(slot, 1, 9, x_last))
        begin(ag_copy(slot, 10, core_peer))

    def ag_relay_far():
        slot = near(2, 0)
        ag_half(slot, 0, 0, core_peer).wait_recv()
        ag_half(slot, 1, 0, core_peer).wait_recv()
        begin(ag_copy(slot, 11, y_peer))
        begin(ag_copy(slot, 12, core_peer))
        for index, slot in ((13, near(3, 1)), (14, near(1, 1)), (15, near(2, 1))):
            ag_wait(slot)
            begin(ag_copy(slot, index, core_peer))

    lane = lax.broadcasted_iota(jnp.int32, (ROWS, 128), 1)

    def slot_of(place_index):
        group, i = place_index // 4, place_index % 4
        far, twin = group // 2, group % 2
        d_near = jnp.where(i < 2, 0, jnp.where(i == 2, 3, 1))
        d_far = jnp.where(i < 2, 2, jnp.where(i == 2, 3, 1))
        other_near = jnp.where(i == 1, 1, 0)
        other_far = jnp.where(i == 0, 0, 1)
        d = jnp.where(far == 1, d_far, d_near)
        other = jnp.where(far == 1, other_far, other_near)
        return (lax.rem(x + d, NX) * 2 + lax.rem(yl + other, 2)) * 2 + lax.rem(core + twin, 2)

    def rows_of(place_index):
        return pl.ds(pl.multiple_of(place_index * ROWS, ROWS), ROWS)

    def store_parts(place_index, first_col, last_col, value):
        rows = rows_of(place_index)
        high, low = split(value)
        trace_parts[rows, first_col:last_col] = high
        trace_parts[rows, WIDE + first_col : WIDE + last_col] = low
        trace_parts[rows, 2 * WIDE + first_col : 2 * WIDE + last_col] = high

    def prepare_four(group):
        def prepare(i, carry):
            store_parts(i, 0, 640, traces[slot_of(i)])
            return carry

        lax.fori_loop(4 * group, 4 * group + 4, prepare, 0)

    def transform(rows, first_row):
        def block(i, carry):
            at_rows = pl.ds(first_row, rows)
            cols = pl.ds(pl.multiple_of(i * 256, 256), 256)
            spec[at_rows, cols] = dot(trace_parts[at_rows, :], table_v[:, cols])
            return carry

        lax.fori_loop(0, 5, block, 0)

    def partner(d, other):
        return seg_of(lax.rem(x + d, NX), (1 - yl) if other else yl, 1 - core)

    ag_begin()
    ag_relay_near()
    prepare_four(0)
    for copy in table_copies:
        copy.wait()
    spill_table[...] = jnp.zeros((128, 2 * WIDE), bf16)
    spill_table[0:16, :] = table_v[0:16, :]
    spill_table[16:32, :] = table_v[0:16, :]
    spill_table[32:48, :] = table_v[2 * WIDE : 2 * WIDE + 16, :]
    transform(128, 0)

    row = lax.broadcasted_iota(jnp.int32, (512, 512), 0)
    col = lax.broadcasted_iota(jnp.int32, (512, 512), 1)
    negative = (row > 0) & (row < 256) & (col == MAXLAG - row)
    positive = (row >= 256) & (col == MAXLAG - 256 + row)
    place[...] = jnp.where(negative | positive, 1.0, 0.0).astype(bf16)

    def wait_first(i, carry):
        zs, gs = i // 2, 2 * q + i % 2

        @pl.when(jnp.logical_not((zs == z) & (gs == seg)))
        def _():
            pltpu.make_async_remote_copy(
                src_ref=pick.at[0], dst_ref=first.at[i],
                send_sem=p1_send.at[0], recv_sem=p1_recv.at[i],
                device_id=core_peer, device_id_type=MESH,
            ).wait_recv()

        return carry

    lax.fori_loop(0, 16, wait_first, 0)
    for low in range(2):
        total = first[low]
        for zs in range(1, NZ):
            total = total + first[2 * zs + low]
        second[yh, low] = total

    def second_copy(d):
        return pltpu.make_async_remote_copy(
            src_ref=second.at[yh], dst_ref=second.at[yh],
            send_sem=p2_send.at[d], recv_sem=p2_recv.at[yh],
            device_id=at(z * NYH + lax.rem(yh + d, NYH), seg), device_id_type=MESH,
        )

    for d in (2, 1, 3):
        copy = second_copy(d)
        copy.start()
        started.append(copy)

    for d, other in ((0, 0), (0, 1), (3, 0), (1, 0)):
        ag_wait(partner(d, other))
    prepare_four(1)
    transform(128, 128)
    ag_relay_far()
    prepare_four(2)
    transform(128, 256)

    for d in range(1, NYH):
        slot = lax.rem(yh + d, NYH)
        pltpu.make_async_remote_copy(
            src_ref=second.at[slot], dst_ref=second.at[slot],
            send_sem=p2_send.at[d], recv_sem=p2_recv.at[slot],
            device_id=core_peer, device_id_type=MESH,
        ).wait_recv()
    for low in range(2):
        sources[q, low] = second[0, low] + second[1, low] + second[2, low] + second[3, low]

    def third_copy(slot, index, device):
        return pltpu.make_async_remote_copy(
            src_ref=sources.at[slot], dst_ref=sources.at[slot],
            send_sem=p3_send.at[index], recv_sem=p3_recv.at[slot],
            device_id=device, device_id_type=MESH,
        )

    for d in (4, 3, 5, 2, 6, 1, 7):
        copy = third_copy(q, d, at(lax.rem(z + d, NZ) * NYH + yh, seg))
        copy.start()
        started.append(copy)

    for d, other in ((2, 0), (2, 1), (3, 1), (1, 1)):
        ag_wait(partner(d, other))
    prepare_four(3)

    def place_spill(i, carry):
        g = slot_of(i)
        last = traces[jnp.maximum(g - 1, 0), :, 512:640]
        high, low = split(jnp.where(g > 0, last, 0.0))
        high, low = high.astype(f32), low.astype(f32)
        parts = jnp.where(lane < 15, pltpu.roll(high, 15, 1), 0.0)
        parts = jnp.where((lane >= 16) & (lane < 31), pltpu.roll(low, 31, 1), parts)
        parts = jnp.where((lane >= 32) & (lane < 47), pltpu.roll(high, 47, 1), parts)
        spills[rows_of(i), :] = parts.astype(bf16)
        return carry

    lax.fori_loop(0, SEGS, place_spill, 0)
    transform(128, 384)

    def whiten_rows(g, carry):
        rows = pl.ds(pl.multiple_of(g * 128, 128), 128)
        early = dot(spills[rows, :], spill_table[...])
        re, im = whiten(
            spec[rows, 0:640] + early[:, 0:640], spec[rows, 640:1280] + early[:, 640:1280]
        )
        spec[rows, 0:640] = re
        spec[rows, 640:1280] = im
        return carry

    lax.fori_loop(0, 4, whiten_rows, 0)

    for d in range(1, NZ):
        slot = lax.rem(q + d, NZ)
        third_copy(slot, 0, core_peer).wait_recv()
    for p in range(SEGS):
        g = slot_of(p)
        prev = jnp.maximum(g - 1, 0)
        for e in range(2):
            row = e * 16 + p
            src_rows[row : row + 1, :] = sources[g // 2, g % 2, e : e + 1, :]
            last = sources[prev // 2, prev % 2, e : e + 1, 512:640]
            src_last[row : row + 1, :] = jnp.where(g > 0, last, 0.0)
    spill = jnp.where(lane < 15, pltpu.roll(src_last[...], 15, 1), 0.0)
    whole = jnp.concatenate([src_rows[:, 0:128] + spill, src_rows[:, 128:640]], axis=1)
    s_high, s_low = split(whole)
    s_both = jnp.concatenate([s_high, s_low], axis=0)

    def transform_src(block, carry):
        cols = pl.ds(pl.multiple_of(block * 256, 256), 256)
        pair = dot(s_both, table_v[0:WIDE, cols])
        src_spec[:, cols] = pair[0:32] + pair[32:64] + dot(s_high, table_v[2 * WIDE : 3 * WIDE, cols])
        return carry

    lax.fori_loop(0, 5, transform_src, 0, unroll=True)
    re, im = whiten(src_spec[:, 0:640], src_spec[:, 640:1280])
    src_spec[:, 0:640] = re
    src_spec[:, 640:1280] = im

    factor = 1.0 / math.sqrt(2.0 * SEG_LEN * SEGS)

    def cross_block(block, carry):
        re_cols = pl.ds(pl.multiple_of(block * 128, 128), 128)
        im_cols = pl.ds(pl.multiple_of(640 + block * 128, 128), 128)
        freq = block * 128 + lane
        weight = jnp.where((freq == 0) | (freq == SEG_LEN), factor, 2.0 * factor)
        acc = [[jnp.zeros((ROWS, 128), f32) for _ in range(2)] for _ in range(2)]
        for g in range(SEGS):
            c_re = spec[g * ROWS : g * ROWS + ROWS, re_cols]
            c_im = spec[g * ROWS : g * ROWS + ROWS, im_cols]
            for e in range(2):
                s_re = src_spec[e * 16 + g : e * 16 + g + 1, re_cols]
                s_im = src_spec[e * 16 + g : e * 16 + g + 1, im_cols]
                acc[e][0] = acc[e][0] + (s_re * c_re + s_im * c_im)
                acc[e][1] = acc[e][1] + (s_re * c_im - s_im * c_re)
        for e in range(2):
            cross[e * ROWS : e * ROWS + ROWS, re_cols] = acc[e][0] * weight
            cross[e * ROWS : e * ROWS + ROWS, im_cols] = acc[e][1] * weight
        return carry

    lax.fori_loop(0, 5, cross_block, 0)

    parts = []
    for base in (0, 640):
        c_high, c_low = split(cross[:, base : base + 640])
        pair = dot_t(jnp.concatenate([c_high, c_low], axis=0), table_v[0:256, base : base + 640])
        parts.append(
            pair[0:64] + pair[64:128] + dot_t(c_high, table_v[2 * WIDE : 2 * WIDE + 256, base : base + 640])
        )
    even, odd = parts
    lags = jnp.concatenate([even - odd, even + odd], axis=1)
    l_high, l_low = split(lags)
    l_last = (lags - l_high.astype(f32) - l_low.astype(f32)).astype(bf16)
    moved = dot(jnp.concatenate([l_high, l_low, l_last], axis=0), place[...])
    placed = moved[0:64] + moved[64:128] + moved[128:192]
    for e in range(2):
        out[e] = placed[e * ROWS : e * ROWS + ROWS, 0 : 2 * MAXLAG + 1]

    for copy in started:
        copy.wait_send()

    def wait_send_first(j, carry):
        @pl.when(jnp.logical_not(is_self(j)))
        def _():
            first_copy(j).wait_send()

        return carry

    lax.fori_loop(0, SEGS, wait_send_first, 0)


def body(strain, source_channels):
    vmem = pl.BlockSpec(memory_space=pltpu.VMEM)
    sem = pltpu.SemaphoreType.DMA
    return pl.pallas_call(
        kernel,
        out_shape=jax.ShapeDtypeStruct((2, ROWS, 2 * MAXLAG + 1), f32),
        in_specs=[pl.BlockSpec(memory_space=pl.ANY)] * 4,
        out_specs=vmem,
        scratch_shapes=[
            pltpu.VMEM((ROWS, RAW), f32),
            pltpu.VMEM((1, SOURCES), jnp.int32),
            pltpu.VMEM((2, WIDE, 128), bf16),
            pltpu.VMEM((512, 512), bf16),
            pltpu.VMEM((ROWS, 2688), bf16),
            pltpu.VMEM((ROWS, 2688), bf16),
            pltpu.VMEM((SEGS, ROWS, WIDE), f32),
            pltpu.VMEM((SEGS, 2, WIDE), f32),
            pltpu.VMEM((16, 2, WIDE), f32),
            pltpu.VMEM((NYH, 2, 2, WIDE), f32),
            pltpu.VMEM((NZ, 2, 2, WIDE), f32),
            pltpu.VMEM((SEGS * ROWS, 3 * WIDE), bf16),
            pltpu.VMEM((SEGS * ROWS, 128), bf16),
            pltpu.VMEM((128, 2 * WIDE), bf16),
            pltpu.VMEM((SEGS * ROWS, 2 * WIDE), f32),
            pltpu.VMEM((32, WIDE), f32),
            pltpu.VMEM((32, 128), f32),
            pltpu.VMEM((32, 2 * WIDE), f32),
            pltpu.VMEM((64, 2 * WIDE), f32),
            pltpu.VMEM((3 * WIDE, 2 * WIDE), bf16),
            sem((6,)), sem((16,)), sem((17,)), sem((16,)), sem((16,)),
            sem((4,)), sem((4,)), sem((8,)), sem((8,)),
        ],
        compiler_params=pltpu.CompilerParams(collective_id=0, has_side_effects=True),
        name="noise_stack",
    )(strain, source_channels.reshape(1, SOURCES), jnp.asarray(band_table()), jnp.asarray(forward_table()))


def solution(mesh):
    in_specs = (P("chan", "seg"), P())
    out_specs = P("seg", "chan", None)
    return jax.shard_map(body, mesh=mesh, in_specs=in_specs, out_specs=out_specs, check_vma=False)
```
